256 devices in a mesh: section: 8 (over y, core), dp: 32 (over x, z).
Axes of the slice: x: 4, y: 4, z: 8, core: 2. Of those that a mesh axis runs over, the one named last changes fastest.
Arguments:
- tokens: bfloat16 [4096, 8192], P('dp'), may hold values from -6 to 6
- cotangent: bfloat16 [4096, 8192], P('dp'), may hold values from -9 to 9
- down_weight: bfloat16 [8, 8192, 256], P('section', 'dp'), may hold values from -0.0625 to 0.0625
- up_weight: bfloat16 [8, 8192, 256], P('section', 'dp'), may hold values from -0.0625 to 0.0625
- norm_gain: float32 [8, 8192], P('section'), may hold values from 0.5 to 1.5
- lengths: int32 [32, 4], P('dp'), may hold values from 1 to 96, 128 in all within a row
Outputs:
- fisher: float32 [8, 8192, 256], P('section', 'dp')
The draws below stay inside these ranges and needn't reach their ends.
Inputs may be any that keep to these rules, and one draw needn't show every extreme that they name: Each replica's 4 lengths sum to 128, and the longest in each replica is exactly 96.
All inputs are finite; a program needn't handle non-finite values.
Results may differ from the reference program's by a relative error of at most 0.0039.
Values may be sent and summed in bfloat16 or wider, within the bound.
A program may use at most 64 MiB of HBM per device.

```python
import math
import jax
import jax.numpy as jnp
import numpy as np
from jax import lax

D = 8192
R = 256
TOK_DEV = 128
SEQ_DEV = 4
MAXLEN = 96
SECTIONS = 8
TOKENS = 4096
N_DP = 32


def level_of(stream_key, dims, split, low, high):
    level = 1.0
    for position, blocks in split:
        draws = jax.random.uniform(jax.random.fold_in(jax.random.fold_in(stream_key, 6), position), (blocks,), jnp.float32, low / len(split), high / len(split))
        level = level * jnp.repeat(jnp.exp(draws), dims[position] // blocks).reshape((-1,) + (1,) * (len(dims) - 1 - position))
    return level


def profile(number_of, total, reach, slope):
    portions = [(1 << 20) // math.isqrt(rank ** slope) + 1 for rank in range(2, number_of + 1)]
    rest, holding = total - reach - (number_of - 1), [1] * (number_of - 1)
    while rest > 0:
        movable = [i for i in range(number_of - 1) if holding[i] < reach]
        whole, remaining = sum([portions[i] for i in movable]), rest
        for i in movable:
            extra = min(reach - holding[i], max(1, remaining * portions[i] // whole), rest)
            holding[i] = holding[i] + extra
            rest = rest - extra
    return np.array([reach] + holding)


def uneven_parts(own_key, number_of, total, bound, lean):
    if number_of == 2:
        one = jax.random.randint(own_key, (), max(1, total - bound), min(bound, total - 1) + 1)
        return jnp.stack([one, total - one])
    sizes = jnp.asarray(profile(number_of, total, bound, lean), jnp.int32)
    twos = (number_of - 1) // 2
    source_of, taker = sizes[1:1 + 2 * twos:2], sizes[2:2 + 2 * twos:2]
    room = jnp.minimum(source_of - 1, bound - taker)
    moved = jax.random.randint(jax.random.fold_in(own_key, 1), (twos,), 0, 1 << 20) % (room + 1)
    sizes = sizes.at[1:1 + 2 * twos:2].set(source_of - moved).at[2:2 + 2 * twos:2].set(taker + moved)
    return sizes[jax.random.permutation(jax.random.fold_in(own_key, 2), number_of)]


def bell_draw(key, extent, spread, reach, shards=(), kind=jnp.bfloat16):
    result = spread * jax.random.normal(key, extent, jnp.float32)
    if shards:
        result = result * level_of(key, extent, shards, -0.22, 0.18)
    return jnp.clip(result, -reach, reach).astype(kind)


def setup_inputs(seed: int = 0) -> dict:
    keys = jax.random.split(jax.random.key(seed), 7)
    tokens = bell_draw(keys[0], (TOKENS, D), 1.0, 6.0, ((0, 32),))
    cotangent = bell_draw(keys[1], (TOKENS, D), 1.5, 9.0, ((0, 32),))
    down_weight = bell_draw(keys[2], (SECTIONS, D, R), D ** -0.5, 0.0625, ((0, 8), (1, 32)))
    up_weight = bell_draw(keys[3], (SECTIONS, D, R), D ** -0.5, 0.0625, ((0, 8), (1, 32)))
    norm_gain = jnp.clip(1.0 + 0.1 * jax.random.normal(keys[4], (SECTIONS, D), jnp.float32), 0.5, 1.5)
    lengths = jax.vmap(lambda own: uneven_parts(own, SEQ_DEV, TOK_DEV, MAXLEN, 2))(jax.random.split(keys[5], N_DP)).reshape((N_DP, SEQ_DEV)).astype(jnp.int32)
    return {"tokens": tokens, "cotangent": cotangent, "down_weight": down_weight, "up_weight": up_weight, "norm_gain": norm_gain, "lengths": lengths}


epsilon = 1e-05

def layer_forward(inputs, gain_row, w_down, w_up):
    wide_rows = inputs.astype(jnp.float32)
    inverse_rms = lax.rsqrt(lax.optimization_barrier(jnp.mean(wide_rows * wide_rows, axis=-1, keepdims=True)) + epsilon)
    normed = (wide_rows * inverse_rms * gain_row).astype(jnp.bfloat16)
    pre_act = jnp.dot(normed, w_down, preferred_element_type=jnp.float32)
    activated = jax.nn.silu(pre_act).astype(jnp.bfloat16)
    branch = lax.dot_general(activated, w_up, (((1,), (1,)), ((), ())), preferred_element_type=jnp.float32)
    return (wide_rows + branch).astype(jnp.bfloat16)

def layer_backward(inputs, upstream, gain_row, w_down, w_up):
    wide_rows = inputs.astype(jnp.float32)
    inverse_rms = lax.rsqrt(lax.optimization_barrier(jnp.mean(wide_rows * wide_rows, axis=-1, keepdims=True)) + epsilon)
    normed = (wide_rows * inverse_rms * gain_row).astype(jnp.bfloat16)
    pre_act = jnp.dot(normed, w_down, preferred_element_type=jnp.float32)
    act_grad = jnp.dot(upstream, w_up, preferred_element_type=jnp.float32)
    sigmoid_z = jax.nn.sigmoid(pre_act)
    pre_grad = (act_grad * sigmoid_z * (1.0 + pre_act * (1.0 - sigmoid_z))).astype(jnp.bfloat16)
    norm_grad = lax.dot_general(pre_grad, w_down, (((1,), (1,)), ((), ())), preferred_element_type=jnp.float32)
    gained = norm_grad * gain_row
    inner = lax.optimization_barrier(jnp.mean(wide_rows * gained, axis=-1, keepdims=True))
    input_grad = upstream.astype(jnp.float32) + inverse_rms * (gained - wide_rows * inverse_rms * inverse_rms * inner)
    return (input_grad.astype(jnp.bfloat16), normed, pre_grad)

def fisher_block(normed, pre_grad, lengths):
    offsets = jnp.cumsum(lengths, axis=1) - lengths + (jnp.arange(N_DP, dtype=jnp.int32) * TOK_DEV)[:, None]
    begins = offsets.reshape(-1).astype(jnp.int32)
    counts = lengths.reshape(-1).astype(jnp.int32)
    padded_norm = jnp.concatenate([normed, jnp.zeros((MAXLEN, D), normed.dtype)], axis=0)
    padded_grad = jnp.concatenate([pre_grad, jnp.zeros((MAXLEN, R), pre_grad.dtype)], axis=0)

    def accumulate(fisher_sum, item):
        begin_row, seq_length = item
        window_norm = lax.dynamic_slice_in_dim(padded_norm, begin_row, MAXLEN, 0)
        window_grad = lax.dynamic_slice_in_dim(padded_grad, begin_row, MAXLEN, 0)
        live_rows = jnp.arange(MAXLEN, dtype=jnp.int32) < seq_length
        window_grad = jnp.where(live_rows[:, None], window_grad, jnp.zeros_like(window_grad))
        seq_grad = lax.dot_general(window_norm, window_grad, (((0,), (0,)), ((), ())), preferred_element_type=jnp.float32)
        return (fisher_sum + seq_grad * seq_grad, None)
    fisher_sum = lax.scan(accumulate, jnp.zeros((D, R), jnp.float32), (begins, counts))[0]
    return fisher_sum / TOKENS

def reference(tokens, cotangent, down_weight, up_weight, norm_gain, lengths):
    hidden = tokens
    layer_inputs = []
    for layer_index in range(SECTIONS):
        layer_inputs.append(hidden)
        hidden = layer_forward(hidden, norm_gain[layer_index], down_weight[layer_index], up_weight[layer_index])
    upstream = cotangent
    blocks = [None] * SECTIONS
    for layer_index in reversed(range(SECTIONS)):
        upstream, normed, pre_grad = layer_backward(layer_inputs[layer_index], upstream, norm_gain[layer_index], down_weight[layer_index], up_weight[layer_index])
        blocks[layer_index] = fisher_block(normed, pre_grad, lengths)
    return jnp.stack(blocks)
```

```python
import functools

import jax
import jax.numpy as jnp
from jax import lax
from jax.experimental import pallas as pl
from jax.experimental.pallas import tpu as pltpu
from jax.sharding import Mesh
from jax.sharding import PartitionSpec as P

MESH = pl.DeviceIdType.MESH
F32 = jnp.float32
BF16 = jnp.bfloat16
NX, NZ, NS = 4, 8, 8
B = 256
D = 8192
R = 256
TOK = 128
MB = 16
NM = TOK // MB
EPS = 1e-05
PHASES = 4

GATHER_CHANNELS = 76
RS_CHANNELS = 76


def half(d):
    return pl.ds(0, 128) if d > 0 else pl.ds(128, 128)


def kernel(
    tok, cot, dwn, upw, gain, lens, out,
    wd, wu, hbuf, hout, nbuf, gbuf, gout, prebuf, invbuf, pgbuf, masked, fsum,
    rb_s, rb_r, ra_s, ra_r, gb, ga, sb_s, sb_r, sa_s, sa_r,
    lsem, ssem, grecv, frecv, brecv, rrecv, psem,
):
    s = lax.axis_index("section")
    x = lax.axis_index("x")
    z = lax.axis_index("z")

    def xo(k):
        return lax.rem(x + k + NX, NX)

    def zo(k):
        return lax.rem(z + k + NZ, NZ)

    own = (
        pltpu.make_async_copy(dwn, wd.at[x, z], lsem.at[0]),
        pltpu.make_async_copy(upw, wu.at[x, z], lsem.at[1]),
    )
    for c in own:
        c.start()

    barrier = pltpu.get_barrier_semaphore()
    s_next, s_prev = lax.rem(s + 1, NS), lax.rem(s + NS - 1, NS)
    for where in (
        {"x": xo(1)}, {"x": xo(-1)}, {"z": zo(1)}, {"z": zo(-1)},
        {"section": s_next}, {"section": s_prev},
    ):
        pl.semaphore_signal(barrier, inc=1, device_id=where, device_id_type=MESH)
    pl.semaphore_wait(barrier, 6)

    for c in own:
        c.wait()

    first = pltpu.make_async_copy(tok, hbuf, lsem.at[2])
    last = pltpu.make_async_copy(cot, gbuf, lsem.at[3])

    @pl.when(s == 0)
    def _():
        first.start()

    @pl.when(s == NS - 1)
    def _():
        last.start()

    sent = []
    counter = [0]
    chan = {}

    def number(key):
        if key not in chan:
            chan[key] = counter[0]
            counter[0] += 1
        return chan[key]

    def hop(axis, d):
        return {"x": xo(d)} if axis == "x" else {"z": zo(d)}

    def g_send(key, block, axis, d):
        k = number(key)
        c = pltpu.make_async_remote_copy(
            src_ref=block, dst_ref=block, send_sem=ssem.at[k], recv_sem=grecv.at[k],
            device_id=hop(axis, d), device_id_type=MESH,
        )
        c.start()
        sent.append(c)

    def g_wait(key, block, axis, d):
        k = number(key)
        pltpu.make_async_remote_copy(
            src_ref=block, dst_ref=block, send_sem=ssem.at[k], recv_sem=grecv.at[k],
            device_id=hop(axis, d), device_id_type=MESH,
        ).wait_recv()

    XOFF = (0, -1, 1, 2)
    ZOFF = (0, -1, 1, -2, 2, -3, 3, 4)

    def send_dx():
        for d in (1, -1):
            g_send(("dX", d), wd.at[x, z], "x", d)

    def wait_dx():
        for d in (1, -1):
            g_wait(("dX", d), wd.at[xo(-d), z], "x", d)

    def send_dx2():
        for d in (1, -1):
            g_send(("dX2", d), wd.at[xo(-d), z, half(d)], "x", d)

    def wait_dx2():
        for d in (1, -1):
            g_wait(("dX2", d), wd.at[xo(2), z, half(d)], "x", d)

    def send_uz(j):
        for d in (1, -1):
            blk = wu.at[x, zo(-d * (j - 1))]
            g_send(("uZ", d, j), blk if j < 4 else blk.at[half(d)], "z", d)

    def wait_uz(j):
        for d in (1, -1):
            blk = wu.at[x, zo(-d * j)]
            g_wait(("uZ", d, j), blk if j < 4 else blk.at[half(d)], "z", d)

    def send_dz(j, c):
        for d in (1, -1):
            blk = wd.at[xo(XOFF[c]), zo(-d * (j - 1))]
            g_send(("dZ", d, j, c), blk if j < 4 else blk.at[half(d)], "z", d)

    def wait_dz(j, c):
        for d in (1, -1):
            blk = wd.at[xo(XOFF[c]), zo(-d * j)]
            g_wait(("dZ", d, j, c), blk if j < 4 else blk.at[half(d)], "z", d)

    def send_ux(q):
        for d in (1, -1):
            g_send(("uX", d, q), wu.at[x, zo(ZOFF[q])], "x", d)

    def wait_ux(q):
        for d in (1, -1):
            g_wait(("uX", d, q), wu.at[xo(-d), zo(ZOFF[q])], "x", d)

    def send_ux2(q):
        for d in (1, -1):
            g_send(("uX2", d, q), wu.at[xo(-d), zo(ZOFF[q]), half(d)], "x", d)

    def wait_ux2(q):
        for d in (1, -1):
            g_wait(("uX2", d, q), wu.at[xo(2), zo(ZOFF[q]), half(d)], "x", d)

    def relay_ux(q):
        wait_ux(q)
        send_ux2(q)

    def relay_dz(j, c):
        wait_dz(j, c)
        send_dz(j + 1, c)

    send_dx()
    send_uz(1)
    send_dz(1, 0)
    send_ux(0)
    wait_dx()
    send_dx2()
    send_dz(1, 1)
    send_dz(1, 2)
    wait_uz(1)
    send_uz(2)
    send_ux(1)
    send_ux(2)
    wait_dx2()
    send_dz(1, 3)
    relay_ux(0)
    relay_dz(1, 0)
    wait_uz(2)
    send_uz(3)
    send_ux(3)
    send_ux(4)
    relay_ux(1)
    relay_ux(2)
    relay_dz(1, 1)
    relay_dz(1, 2)
    wait_uz(3)
    send_uz(4)
    send_ux(5)
    send_ux(6)
    relay_dz(1, 3)
    relay_dz(2, 0)
    relay_ux(3)
    relay_ux(4)
    relay_dz(2, 1)
    relay_dz(2, 2)
    wait_uz(4)
    send_ux(7)
    relay_dz(2, 3)
    relay_ux(5)
    relay_ux(6)
    for c in range(4):
        relay_dz(3, c)
    relay_ux(7)
    for c in range(4):
        wait_dz(4, c)
    for q in range(8):
        wait_ux2(q)
    for c in sent:
        c.wait_send()
    sent.clear()

    @pl.when(s == 0)
    def _():
        first.wait()

    @pl.when(s == NS - 1)
    def _():
        last.wait()

    def f_copy(i):
        return pltpu.make_async_remote_copy(
            src_ref=hout.at[i], dst_ref=hbuf.at[i], send_sem=psem.at[0, i], recv_sem=frecv.at[i],
            device_id={"section": s_next}, device_id_type=MESH,
        )

    def b_copy(i):
        return pltpu.make_async_remote_copy(
            src_ref=gout.at[i], dst_ref=gbuf.at[i], send_sem=psem.at[1, i], recv_sem=brecv.at[i],
            device_id={"section": s_prev}, device_id_type=MESH,
        )

    def blk(r):
        return slice(r * B, (r + 1) * B)

    def forward(i, carry):
        @pl.when(s > 0)
        def _():
            f_copy(i).wait_recv()

        rows = pl.ds(pl.multiple_of(i * MB, MB), MB)
        squares = jnp.zeros((MB, B), F32)
        for r in range(NX * NZ):
            h = hbuf[i, :, blk(r)].astype(F32)
            squares = squares + h * h
        inv = lax.rsqrt(jnp.sum(squares, axis=-1, keepdims=True) * (1.0 / D) + EPS)
        acc = jnp.zeros((MB, R), F32)
        for r in range(NX * NZ):
            h = hbuf[i, :, blk(r)].astype(F32)
            n = (h * inv * gain[:, blk(r)]).astype(BF16)
            nbuf[rows, blk(r)] = n
            acc = acc + jnp.dot(n, wd[r // NZ, r % NZ], preferred_element_type=F32)
        prebuf[rows, :] = acc
        invbuf[rows, :] = jnp.broadcast_to(inv, (MB, 128))
        act = (acc * jax.nn.sigmoid(acc)).astype(BF16)

        @pl.when(s < NS - 1)
        def _():
            for r in range(NX * NZ):
                up = lax.dot_general(
                    act, wu[r // NZ, r % NZ], (((1,), (1,)), ((), ())), preferred_element_type=F32
                )
                hout[i, :, blk(r)] = (hbuf[i, :, blk(r)].astype(F32) + up).astype(BF16)
            f_copy(i).start()

        return carry

    if PHASES >= 2:
        lax.fori_loop(0, NM, forward, 0)

    def backward(i, carry):
        @pl.when(s < NS - 1)
        def _():
            b_copy(i).wait_recv()

        rows = pl.ds(pl.multiple_of(i * MB, MB), MB)
        acc = jnp.zeros((MB, R), F32)
        for r in range(NX * NZ):
            acc = acc + jnp.dot(
                gbuf[i, :, blk(r)], wu[r // NZ, r % NZ], preferred_element_type=F32
            )
        pre = prebuf[rows, :]
        sig = jax.nn.sigmoid(pre)
        pg = (acc * sig * (1.0 + pre * (1.0 - sig))).astype(BF16)
        pgbuf[rows, :] = pg

        @pl.when(s > 0)
        def _():
            inv = invbuf[rows, 0:1]
            inner = jnp.sum(pg.astype(F32) * pre, axis=-1, keepdims=True) * (1.0 / D)
            coef = inv * inv * inner
            for r in range(NX * NZ):
                q = lax.dot_general(
                    pg, wd[r // NZ, r % NZ], (((1,), (1,)), ((), ())), preferred_element_type=F32
                )
                g = gbuf[i, :, blk(r)].astype(F32) + (
                    inv * (q * gain[:, blk(r)]) - coef * hbuf[i, :, blk(r)].astype(F32)
                )
                gout[i, :, blk(r)] = g.astype(BF16)
            b_copy(i).start()

        return carry

    if PHASES >= 3:
        lax.fori_loop(0, NM, backward, 0)

    if PHASES >= 2:
        @pl.when(s < NS - 1)
        def _():
            @pl.loop(0, NM)
            def _(i):
                f_copy(i).wait_send()

    if PHASES >= 3:
        @pl.when(s > 0)
        def _():
            @pl.loop(0, NM)
            def _(i):
                b_copy(i).wait_send()

    if PHASES < 4:
        out[...] = jnp.zeros((1, B, R), F32)
        return

    pgt = pgbuf[...].astype(F32).T
    position = lax.broadcasted_iota(jnp.int32, (1, TOK), 1)
    start = jnp.int32(0)
    for j in range(4):
        end = start + lens[0, j]
        inside = (position >= start) & (position < end)
        masked[j * R : (j + 1) * R, :] = jnp.where(inside, pgt, 0.0).astype(BF16)
        start = end

    for a in range(NX):
        @pl.loop(0, NZ)
        def _(b, a=a):
            cols = pl.ds(pl.multiple_of((a * NZ + b) * B, B), B)
            p = jnp.dot(masked[...], nbuf[:, cols], preferred_element_type=F32)
            p = p * p
            fsum[a, b] = (p[0:R] + p[R : 2 * R]) + (p[2 * R : 3 * R] + p[3 * R : 4 * R])

    rcount = [0]
    rchan = {}

    def rnumber(key):
        if key not in rchan:
            rchan[key] = rcount[0]
            rcount[0] += 1
        return rchan[key]

    def r_copy(key, src, dst, axis, d):
        k = rnumber(key)
        return pltpu.make_async_remote_copy(
            src_ref=src, dst_ref=dst, send_sem=ssem.at[k], recv_sem=rrecv.at[k],
            device_id=hop(axis, d), device_id_type=MESH,
        )

    def go(c):
        c.start()
        sent.append(c)

    def side(d):
        return 0 if d > 0 else 1

    def part(d):
        return slice(0, 64) if d > 0 else slice(64, 128)

    HALF, FULL = pl.ds(0, 64), pl.ds(0, 128)

    def ring(key, axis, depth, mine, sbuf, rbuf, d, j):
        e = side(d)
        span = HALF if j == depth else FULL
        value = mine(j * d)
        if j == depth:
            sbuf[e, j - 1, 0:64] = value[part(d)].astype(BF16)
        else:
            if j == depth - 1:
                r_copy(key + (d, j + 1), sbuf.at[e, j, HALF], rbuf.at[e, j, HALF], axis, d).wait_recv()
                got = rbuf[e, j, 0:64].astype(F32)
                fresh = part(d).start
                keep = 64 - fresh
                sbuf[e, j - 1, fresh : fresh + 64] = (value[part(d)] + got).astype(BF16)
                sbuf[e, j - 1, keep : keep + 64] = value[keep : keep + 64].astype(BF16)
            else:
                r_copy(key + (d, j + 1), sbuf.at[e, j, FULL], rbuf.at[e, j, FULL], axis, d).wait_recv()
                sbuf[e, j - 1] = (value + rbuf[e, j].astype(F32)).astype(BF16)
        go(r_copy(key + (d, j), sbuf.at[e, j - 1, span], rbuf.at[e, j - 1, span], axis, d))

    def ring_end(key, axis, mine, sbuf, rbuf):
        value = mine(0)
        for d in (1, -1):
            e = side(d)
            r_copy(key + (d, 1), sbuf.at[e, 0, FULL], rbuf.at[e, 0, FULL], axis, d).wait_recv()
            value = value + rbuf[e, 0].astype(F32)
        return value

    def stage_a(q, d, j):
        ring(("A1", q), "x", 2, lambda k: fsum[xo(k), q, 0:128], ra_s.at[q], ra_r.at[q], d, j)

    def stage_b(c, d, j):
        ring(("B1", c), "z", 4, lambda k: fsum[c, zo(k), 128:256], rb_s.at[c], rb_r.at[c], d, j)

    for c in range(NX):
        for d in (1, -1):
            stage_b(c, d, 4)
    for q in range(NZ):
        for d in (1, -1):
            stage_a(q, d, 2)
    for c in range(NX):
        for d in (1, -1):
            stage_b(c, d, 3)
    for q in range(NZ):
        for d in (1, -1):
            stage_a(q, d, 1)
    for c in range(NX):
        for d in (1, -1):
            stage_b(c, d, 2)
    for c in range(NX):
        for d in (1, -1):
            stage_b(c, d, 1)
    for q in range(NZ):
        ga[q] = ring_end(("A1", q), "x", lambda k: fsum[xo(k), q, 0:128], ra_s.at[q], ra_r.at[q])

    def last_a(d, j):
        ring(("A2",), "z", 4, lambda k: ga[zo(k)], sa_s, sa_r, d, j)

    def last_b(d, j):
        ring(("B2",), "x", 2, lambda k: gb[xo(k)], sb_s, sb_r, d, j)

    for d in (1, -1):
        last_a(d, 4)
    for c in range(NX):
        gb[c] = ring_end(("B1", c), "z", lambda k: fsum[c, zo(k), 128:256], rb_s.at[c], rb_r.at[c])
    for d in (1, -1):
        last_b(d, 2)
    for d in (1, -1):
        last_a(d, 3)
    for d in (1, -1):
        last_b(d, 1)
    for j in (2, 1):
        for d in (1, -1):
            last_a(d, j)
    low = ring_end(("A2",), "z", lambda k: ga[zo(k)], sa_s, sa_r)
    high = ring_end(("B2",), "x", lambda k: gb[xo(k)], sb_s, sb_r)
    scale = 1.0 / (TOK * NX * NZ)
    out[0, :, 0:128] = low.T * scale
    out[0, :, 128:256] = high.T * scale
    for c in sent:
        c.wait_send()


def per_device(tokens, cotangent, down_weight, up_weight, norm_gain, lengths):
    hbm = pl.BlockSpec(memory_space=pl.ANY)
    vmem = pl.BlockSpec(memory_space=pltpu.VMEM)
    dma = pltpu.SemaphoreType.DMA
    return pl.pallas_call(
        kernel,
        out_shape=jax.ShapeDtypeStruct((1, B, R), F32),
        in_specs=[hbm, hbm, hbm, hbm, vmem, pl.BlockSpec(memory_space=pltpu.SMEM)],
        out_specs=vmem,
        scratch_shapes=[
            pltpu.VMEM((NX, NZ, B, R), BF16),
            pltpu.VMEM((NX, NZ, B, R), BF16),
            pltpu.VMEM((NM, MB, D), BF16),
            pltpu.VMEM((NM, MB, D), BF16),
            pltpu.VMEM((TOK, D), BF16),
            pltpu.VMEM((NM, MB, D), BF16),
            pltpu.VMEM((NM, MB, D), BF16),
            pltpu.VMEM((TOK, R), F32),
            pltpu.VMEM((TOK, 128), F32),
            pltpu.VMEM((TOK, R), BF16),
            pltpu.VMEM((4 * R, TOK), BF16),
            pltpu.VMEM((NX, NZ, R, B), F32),
            pltpu.VMEM((NX, 2, 4, 128, B), BF16),
            pltpu.VMEM((NX, 2, 4, 128, B), BF16),
            pltpu.VMEM((NZ, 2, 2, 128, B), BF16),
            pltpu.VMEM((NZ, 2, 2, 128, B), BF16),
            pltpu.VMEM((NX, 128, B), F32),
            pltpu.VMEM((NZ, 128, B), F32),
            pltpu.VMEM((2, 2, 128, B), BF16),
            pltpu.VMEM((2, 2, 128, B), BF16),
            pltpu.VMEM((2, 4, 128, B), BF16),
            pltpu.VMEM((2, 4, 128, B), BF16),
            dma((4,)),
            dma((GATHER_CHANNELS,)),
            dma((GATHER_CHANNELS,)),
            dma((NM,)),
            dma((NM,)),
            dma((RS_CHANNELS,)),
            dma((2, NM)),
        ],
        compiler_params=pltpu.CompilerParams(
            collective_id=0, has_side_effects=True, vmem_limit_bytes=62 * 1024 * 1024
        ),
    )(
        tokens.reshape(NM, MB, D),
        cotangent.reshape(NM, MB, D),
        down_weight[0],
        up_weight[0],
        norm_gain,
        lengths,
    )


def solution(mesh):
    split = Mesh(mesh.devices.reshape(NS, NX, NZ), ("section", "x", "z"))
    dp = ("x", "z")
    return jax.shard_map(
        per_device,
        mesh=split,
        in_specs=(
            P(dp, None),
            P(dp, None),
            P("section", dp, None),
            P("section", dp, None),
            P("section", None),
            P(dp, None),
        ),
        out_specs=P("section", dp, None),
        check_vma=False,
    )
```

```python
import functools

import jax
import jax.numpy as jnp
from jax import lax
from jax.experimental import pallas as pl
from jax.experimental.pallas import tpu as pltpu
from jax.sharding import Mesh
from jax.sharding import PartitionSpec as P

MESH = pl.DeviceIdType.MESH
F32 = jnp.float32
BF16 = jnp.bfloat16
NX, NZ, NS = 4, 8, 8
B = 256
D = 8192
R = 256
TOK = 128
MB = 16
NM = TOK // MB
EPS = 1e-05

GATHER_CHANNELS = 76
RS_CHANNELS = 76


def half(d):
    return pl.ds(0, 128) if d > 0 else pl.ds(128, 128)


def kernel(
    tok, cot, dwn, upw, gain, lens, out,
    wd, wu, hbuf, hout, nbuf, cbuf, ebuf, mat, msg, gacc, hup, csum, actbuf, prebuf, invbuf, pgbuf, masked, fsum,
    rb_s, rb_r, ra_s, ra_r, gb, ga, sb_s, sb_r, sa_s, sa_r,
    lsem, ssem, grecv, frecv, brecv, rrecv, psem, bsend, esend, erecv, zsend, zrecv, xsend, xrecv,
):
    s = lax.axis_index("section")
    x = lax.axis_index("x")
    z = lax.axis_index("z")

    def xo(k):
        return lax.rem(x + k + NX, NX)

    def zo(k):
        return lax.rem(z + k + NZ, NZ)

    own = (
        pltpu.make_async_copy(dwn, wd.at[x, z], lsem.at[0]),
        pltpu.make_async_copy(upw, wu.at[x, z], lsem.at[1]),
    )
    for c in own:
        c.start()

    barrier = pltpu.get_barrier_semaphore()
    s_next, s_prev = lax.rem(s + 1, NS), lax.rem(s + NS - 1, NS)
    for where in (
        {"x": xo(1)}, {"x": xo(-1)}, {"z": zo(1)}, {"z": zo(-1)},
        *({"section": lax.rem(s + k, NS)} for k in range(1, NS)),
    ):
        pl.semaphore_signal(barrier, inc=1, device_id=where, device_id_type=MESH)
    pl.semaphore_wait(barrier, 3 + NS)

    for c in own:
        c.wait()

    first = pltpu.make_async_copy(tok, hbuf, lsem.at[2])
    cotangent = pltpu.make_async_copy(cot, cbuf, lsem.at[3])
    cotangent.start()

    def clear(j, carry):
        ebuf[j] = jnp.zeros((16, D), BF16)
        return carry

    lax.fori_loop(0, s + 1, clear, 0)

    @pl.when(s == 0)
    def _():
        first.start()

    sent = []
    counter = [0]
    chan = {}

    def number(key):
        if key not in chan:
            chan[key] = counter[0]
            counter[0] += 1
        return chan[key]

    def hop(axis, d):
        return {"x": xo(d)} if axis == "x" else {"z": zo(d)}

    def g_send(key, block, axis, d):
        k = number(key)
        c = pltpu.make_async_remote_copy(
            src_ref=block, dst_ref=block, send_sem=ssem.at[k], recv_sem=grecv.at[k],
            device_id=hop(axis, d), device_id_type=MESH,
        )
        c.start()
        sent.append(c)

    def g_wait(key, block, axis, d):
        k = number(key)
        pltpu.make_async_remote_copy(
            src_ref=block, dst_ref=block, send_sem=ssem.at[k], recv_sem=grecv.at[k],
            device_id=hop(axis, d), device_id_type=MESH,
        ).wait_recv()

    XOFF = (0, -1, 1, 2)
    ZOFF = (0, -1, 1, -2, 2, -3, 3, 4)

    def send_dx():
        for d in (1, -1):
            g_send(("dX", d), wd.at[x, z], "x", d)

    def wait_dx():
        for d in (1, -1):
            g_wait(("dX", d), wd.at[xo(-d), z], "x", d)

    def send_dx2():
        for d in (1, -1):
            g_send(("dX2", d), wd.at[xo(-d), z, half(d)], "x", d)

    def wait_dx2():
        for d in (1, -1):
            g_wait(("dX2", d), wd.at[xo(2), z, half(d)], "x", d)

    def send_uz(j):
        for d in (1, -1):
            blk = wu.at[x, zo(-d * (j - 1))]
            g_send(("uZ", d, j), blk if j < 4 else blk.at[half(d)], "z", d)

    def wait_uz(j):
        for d in (1, -1):
            blk = wu.at[x, zo(-d * j)]
            g_wait(("uZ", d, j), blk if j < 4 else blk.at[half(d)], "z", d)

    def send_dz(j, c):
        for d in (1, -1):
            blk = wd.at[xo(XOFF[c]), zo(-d * (j - 1))]
            g_send(("dZ", d, j, c), blk if j < 4 else blk.at[half(d)], "z", d)

    def wait_dz(j, c):
        for d in (1, -1):
            blk = wd.at[xo(XOFF[c]), zo(-d * j)]
            g_wait(("dZ", d, j, c), blk if j < 4 else blk.at[half(d)], "z", d)

    def send_ux(q):
        for d in (1, -1):
            g_send(("uX", d, q), wu.at[x, zo(ZOFF[q])], "x", d)

    def wait_ux(q):
        for d in (1, -1):
            g_wait(("uX", d, q), wu.at[xo(-d), zo(ZOFF[q])], "x", d)

    def send_ux2(q):
        for d in (1, -1):
            g_send(("uX2", d, q), wu.at[xo(-d), zo(ZOFF[q]), half(d)], "x", d)

    def wait_ux2(q):
        for d in (1, -1):
            g_wait(("uX2", d, q), wu.at[xo(2), zo(ZOFF[q]), half(d)], "x", d)

    def relay_ux(q):
        wait_ux(q)
        send_ux2(q)

    def relay_dz(j, c):
        wait_dz(j, c)
        send_dz(j + 1, c)

    send_dx()
    send_uz(1)
    send_dz(1, 0)
    send_ux(0)
    wait_dx()
    send_dx2()
    send_dz(1, 1)
    send_dz(1, 2)
    wait_uz(1)
    send_uz(2)
    send_ux(1)
    send_ux(2)
    wait_dx2()
    send_dz(1, 3)
    relay_ux(0)
    relay_dz(1, 0)
    wait_uz(2)
    send_uz(3)
    send_ux(3)
    send_ux(4)
    relay_ux(1)
    relay_ux(2)
    relay_dz(1, 1)
    relay_dz(1, 2)
    wait_uz(3)
    send_uz(4)
    send_ux(5)
    send_ux(6)
    relay_dz(1, 3)
    relay_dz(2, 0)
    relay_ux(3)
    relay_ux(4)
    relay_dz(2, 1)
    relay_dz(2, 2)
    wait_uz(4)
    send_ux(7)
    relay_dz(2, 3)
    relay_ux(5)
    relay_ux(6)
    for c in range(4):
        relay_dz(3, c)
    relay_ux(7)
    for c in range(4):
        wait_dz(4, c)
    for q in range(8):
        wait_ux2(q)
    for c in sent:
        c.wait_send()
    sent.clear()

    @pl.when(s == 0)
    def _():
        first.wait()

    LATE = 6
    EARLY = 4

    def blk(r):
        return slice(r * B, (r + 1) * B)

    replica = x * NZ + z

    def e_copy(j, below):
        return pltpu.make_async_remote_copy(
            src_ref=ebuf.at[j], dst_ref=ebuf.at[j], send_sem=esend.at[below], recv_sem=erecv.at[j],
            device_id={"section": below}, device_id_type=MESH,
        )

    @pl.when(s > 0)
    def _():
        pick = lax.broadcasted_iota(jnp.int32, (8, R), 1) == (
            lax.broadcasted_iota(jnp.int32, (8, R), 0) + replica * 8
        )
        pick = jnp.where(pick, 1.0, 0.0).astype(BF16)
        for r in range(NX * NZ):
            rows_d = lax.dot_general(
                pick, wd[r // NZ, r % NZ], (((1,), (1,)), ((), ())), preferred_element_type=F32
            )
            rows_u = lax.dot_general(
                pick, wu[r // NZ, r % NZ], (((1,), (1,)), ((), ())), preferred_element_type=F32
            )
            ebuf[s, :, blk(r)] = jnp.concatenate([rows_d * gain[:, blk(r)], rows_u], axis=0).astype(BF16)

        def offer(t, carry):
            e_copy(s, s - 1 - t).start()
            return carry

        lax.fori_loop(0, s, offer, 0)

    def z_copy(j, h, d, arriving):
        k = zo(-d * h) if arriving else zo(-d * (h - 1))
        e = 0 if d > 0 else 1
        ref = mat.at[j, :, x, k] if h < 4 else mat.at[j, e, x, k]
        return pltpu.make_async_remote_copy(
            src_ref=ref, dst_ref=ref, send_sem=zsend.at[j, 2 * h - 2 + e], recv_sem=zrecv.at[j, 2 * h - 2 + e],
            device_id={"z": zo(d)}, device_id_type=MESH,
        )

    def x_copy(j, h, d, arriving):
        k = xo(-d * h) if arriving else xo(-d * (h - 1))
        e = 0 if d > 0 else 1
        ref = mat.at[j, :, k] if h < 2 else mat.at[j, e, k]
        return pltpu.make_async_remote_copy(
            src_ref=ref, dst_ref=ref, send_sem=xsend.at[j, 2 * h - 2 + e], recv_sem=xrecv.at[j, 2 * h - 2 + e],
            device_id={"x": xo(d)}, device_id_type=MESH,
        )

    def above(body):
        def step(t, carry):
            body(s + 1 + t)
            return carry

        lax.fori_loop(0, NS - 1 - s, step, 0)

    def exchange_begin():
        above(lambda j: e_copy(j, s_prev).wait_recv())
        acc = jnp.zeros((NS * 16, R), F32)
        for r in range(NX * NZ):
            rows_e = ebuf[:, :, blk(r)].reshape(NS * 16, B)
            acc = acc + jnp.dot(rows_e, wu[r // NZ, r % NZ], preferred_element_type=F32)
        for j in range(1, NS):
            mat[j, 0, x, z] = acc[16 * j : 16 * j + 8].astype(BF16)
            mat[j, 1, x, z] = acc[16 * j + 8 : 16 * j + 16].astype(BF16)

        def begin(j):
            for d in (1, -1):
                z_copy(j, 1, d, False).start()

        above(begin)

    def along(h):
        def on(j):
            for d in (1, -1):
                z_copy(j, h, d, True).wait_recv()
            for d in (1, -1):
                z_copy(j, h + 1, d, False).start()

        above(on)

    def turn():
        def one(j):
            for d in (1, -1):
                z_copy(j, 4, d, True).wait_recv()
            for d in (1, -1):
                x_copy(j, 1, d, False).start()

        above(one)

    def across():
        def one(j):
            for d in (1, -1):
                x_copy(j, 1, d, True).wait_recv()
            for d in (1, -1):
                x_copy(j, 2, d, False).start()

        above(one)

    def finish():
        def one(j):
            for d in (1, -1):
                x_copy(j, 2, d, True).wait_recv()

        above(one)

    exchange_steps = (
        lambda: along(1), lambda: along(2), lambda: along(3), turn, across, finish,
    )

    def exchange_sent():
        def one(j):
            for d in (1, -1):
                for h in (1, 2, 3, 4):
                    z_copy(j, h, d, False).wait_send()
                for h in (1, 2):
                    x_copy(j, h, d, False).wait_send()

        above(one)

    def start_gradient():
        cotangent.wait()
        acc = jnp.zeros((TOK, R), F32)
        for r in range(NX * NZ):
            acc = acc + jnp.dot(cbuf[:, blk(r)], wu[r // NZ, r % NZ], preferred_element_type=F32)
        gacc[...] = acc

    @pl.when(s >= LATE)
    def _():
        start_gradient()

    @pl.when((s > EARLY) & (s < NS - 1))
    def _():
        exchange_begin()

    def micro(i):
        return pl.ds(pl.multiple_of(i * MB, MB), MB)

    def f_copy(i):
        return pltpu.make_async_remote_copy(
            src_ref=hout.at[micro(i)], dst_ref=hbuf.at[micro(i)], send_sem=psem.at[i], recv_sem=frecv.at[i],
            device_id={"section": s_next}, device_id_type=MESH,
        )

    def forward(i, carry):
        @pl.when(s > 0)
        def _():
            f_copy(i).wait_recv()

        rows = micro(i)
        squares = jnp.zeros((MB, B), F32)
        for r in range(NX * NZ):
            h = hbuf[rows, blk(r)].astype(F32)
            squares = squares + h * h
        inv = lax.rsqrt(jnp.sum(squares, axis=-1, keepdims=True) * (1.0 / D) + EPS)
        acc = jnp.zeros((MB, R), F32)
        for r in range(NX * NZ):
            h = hbuf[rows, blk(r)].astype(F32)
            n = (h * inv * gain[:, blk(r)]).astype(BF16)
            nbuf[rows, blk(r)] = n
            acc = acc + jnp.dot(n, wd[r // NZ, r % NZ], preferred_element_type=F32)
        prebuf[rows, :] = acc
        invbuf[rows, :] = jnp.broadcast_to(inv, (MB, 128))
        act = (acc * jax.nn.sigmoid(acc)).astype(BF16)
        actbuf[rows, :] = act

        @pl.when(s < NS - 1)
        def _():
            for r in range(NX * NZ):
                up = lax.dot_general(
                    act, wu[r // NZ, r % NZ], (((1,), (1,)), ((), ())), preferred_element_type=F32
                )
                hout[rows, blk(r)] = (hbuf[rows, blk(r)].astype(F32) + up).astype(BF16)
            f_copy(i).start()

        @pl.when((s >= EARLY) & (s < NS - 1))
        def _():
            @pl.when((s == EARLY) & (i == 1))
            def _():
                exchange_begin()

            for k, step in enumerate(exchange_steps):
                pl.when(i == jnp.where(s == EARLY, k + 2, k))(step)

        return carry

    lax.fori_loop(0, NM, forward, 0)

    @pl.when(s < LATE)
    def _():
        start_gradient()

    @pl.when(s < EARLY)
    def _():
        exchange_begin()
        for step in exchange_steps:
            step()

    @pl.when(s < NS - 1)
    def _():
        acc = jnp.zeros((TOK, R), F32)
        for r in range(NX * NZ):
            acc = acc + jnp.dot(hout[:, blk(r)], wu[r // NZ, r % NZ], preferred_element_type=F32)
        hup[...] = acc

    csum[...] = jnp.zeros((TOK, 128), F32)

    def b_copy(j):
        return pltpu.make_async_remote_copy(
            src_ref=msg.at[j], dst_ref=msg.at[j], send_sem=bsend.at[j], recv_sem=brecv.at[j],
            device_id={"section": s_prev}, device_id_type=MESH,
        )

    def arrive(t, carry):
        j = NS - 1 - t
        b_copy(j).wait_recv()

        @pl.when(s > 0)
        def _():
            b_copy(j).start()

        c = msg[j, :, 2 * R : 2 * R + 128].astype(F32)
        csum[...] += c
        from_down = jnp.dot(
            msg[j, :, 0:R], mat[j, 0].reshape(R, R), preferred_element_type=F32
        )
        from_up = jnp.dot(
            msg[j, :, R : 2 * R], mat[j, 1].reshape(R, R), preferred_element_type=F32
        )
        both = jnp.concatenate([c, c], axis=1)
        gacc[...] += from_down + from_up - both * hup[...]
        return carry

    lax.fori_loop(0, NS - 1 - s, arrive, 0)

    pre = prebuf[...]
    sig = jax.nn.sigmoid(pre)
    pg = (gacc[...] * sig * (1.0 + pre * (1.0 - sig))).astype(BF16)
    pgbuf[...] = pg

    @pl.when(s > 0)
    def _():
        wide = pg.astype(F32)
        inv = invbuf[:, 0:1]
        coef = inv * inv * (jnp.sum(wide * pre, axis=-1, keepdims=True) * (1.0 / D))
        msg[s, :, 0:R] = (wide * inv).astype(BF16)
        msg[s, :, R : 2 * R] = (actbuf[...].astype(F32) * (-csum[:, 0:1])).astype(BF16)
        msg[s, :, 2 * R : 2 * R + 128] = jnp.broadcast_to(coef, (TOK, 128)).astype(BF16)
        b_copy(s).start()

    pgt = pgbuf[...].astype(F32).T
    position = lax.broadcasted_iota(jnp.int32, (1, TOK), 1)
    start = jnp.int32(0)
    for j in range(4):
        end = start + lens[0, j]
        inside = (position >= start) & (position < end)
        masked[j * R : (j + 1) * R, :] = jnp.where(inside, pgt, 0.0).astype(BF16)
        start = end

    for a in range(NX):
        @pl.loop(0, NZ)
        def _(b, a=a):
            cols = pl.ds(pl.multiple_of((a * NZ + b) * B, B), B)
            p = jnp.dot(masked[...], nbuf[:, cols], preferred_element_type=F32)
            p = p * p
            fsum[a, b] = (p[0:R] + p[R : 2 * R]) + (p[2 * R : 3 * R] + p[3 * R : 4 * R])

    rcount = [0]
    rchan = {}

    def rnumber(key):
        if key not in rchan:
            rchan[key] = rcount[0]
            rcount[0] += 1
        return rchan[key]

    def r_copy(key, src, dst, axis, d):
        k = rnumber(key)
        return pltpu.make_async_remote_copy(
            src_ref=src, dst_ref=dst, send_sem=ssem.at[k], recv_sem=rrecv.at[k],
            device_id=hop(axis, d), device_id_type=MESH,
        )

    def go(c):
        c.start()
        sent.append(c)

    def side(d):
        return 0 if d > 0 else 1

    def part(d):
        return slice(0, 64) if d > 0 else slice(64, 128)

    HALF, FULL = pl.ds(0, 64), pl.ds(0, 128)

    def ring(key, axis, depth, mine, sbuf, rbuf, d, j):
        e = side(d)
        span = HALF if j == depth else FULL
        value = mine(j * d)
        if j == depth:
            sbuf[e, j - 1, 0:64] = value[part(d)].astype(BF16)
        else:
            if j == depth - 1:
                r_copy(key + (d, j + 1), sbuf.at[e, j, HALF], rbuf.at[e, j, HALF], axis, d).wait_recv()
                got = rbuf[e, j, 0:64].astype(F32)
                fresh = part(d).start
                keep = 64 - fresh
                sbuf[e, j - 1, fresh : fresh + 64] = (value[part(d)] + got).astype(BF16)
                sbuf[e, j - 1, keep : keep + 64] = value[keep : keep + 64].astype(BF16)
            else:
                r_copy(key + (d, j + 1), sbuf.at[e, j, FULL], rbuf.at[e, j, FULL], axis, d).wait_recv()
                sbuf[e, j - 1] = (value + rbuf[e, j].astype(F32)).astype(BF16)
        go(r_copy(key + (d, j), sbuf.at[e, j - 1, span], rbuf.at[e, j - 1, span], axis, d))

    def ring_end(key, axis, mine, sbuf, rbuf):
        value = mine(0)
        for d in (1, -1):
            e = side(d)
            r_copy(key + (d, 1), sbuf.at[e, 0, FULL], rbuf.at[e, 0, FULL], axis, d).wait_recv()
            value = value + rbuf[e, 0].astype(F32)
        return value

    def stage_a(q, d, j):
        ring(("A1", q), "x", 2, lambda k: fsum[xo(k), q, 0:128], ra_s.at[q], ra_r.at[q], d, j)

    def stage_b(c, d, j):
        ring(("B1", c), "z", 4, lambda k: fsum[c, zo(k), 128:256], rb_s.at[c], rb_r.at[c], d, j)

    for c in range(NX):
        for d in (1, -1):
            stage_b(c, d, 4)
    for q in range(NZ):
        for d in (1, -1):
            stage_a(q, d, 2)
    for c in range(NX):
        for d in (1, -1):
            stage_b(c, d, 3)
    for q in range(NZ):
        for d in (1, -1):
            stage_a(q, d, 1)
    for c in range(NX):
        for d in (1, -1):
            stage_b(c, d, 2)
    for c in range(NX):
        for d in (1, -1):
            stage_b(c, d, 1)
    for q in range(NZ):
        ga[q] = ring_end(("A1", q), "x", lambda k: fsum[xo(k), q, 0:128], ra_s.at[q], ra_r.at[q])

    def last_a(d, j):
        ring(("A2",), "z", 4, lambda k: ga[zo(k)], sa_s, sa_r, d, j)

    def last_b(d, j):
        ring(("B2",), "x", 2, lambda k: gb[xo(k)], sb_s, sb_r, d, j)

    for d in (1, -1):
        last_a(d, 4)
    for c in range(NX):
        gb[c] = ring_end(("B1", c), "z", lambda k: fsum[c, zo(k), 128:256], rb_s.at[c], rb_r.at[c])
    for d in (1, -1):
        last_b(d, 2)
    for d in (1, -1):
        last_a(d, 3)
    for d in (1, -1):
        last_b(d, 1)
    for j in (2, 1):
        for d in (1, -1):
            last_a(d, j)
    low = ring_end(("A2",), "z", lambda k: ga[zo(k)], sa_s, sa_r)
    high = ring_end(("B2",), "x", lambda k: gb[xo(k)], sb_s, sb_r)
    scale = 1.0 / (TOK * NX * NZ)
    out[0, :, 0:128] = low.T * scale
    out[0, :, 128:256] = high.T * scale
    for c in sent:
        c.wait_send()

    exchange_sent()

    @pl.when(s < NS - 1)
    def _():
        @pl.loop(0, NM)
        def _(i):
            f_copy(i).wait_send()

    @pl.when(s > 0)
    def _():
        def done(t, carry):
            b_copy(s + t).wait_send()
            return carry

        lax.fori_loop(0, NS - s, done, 0)

        def offered(t, carry):
            e_copy(s, t).wait_send()
            return carry

        lax.fori_loop(0, s, offered, 0)


def per_device(tokens, cotangent, down_weight, up_weight, norm_gain, lengths):
    hbm = pl.BlockSpec(memory_space=pl.ANY)
    vmem = pl.BlockSpec(memory_space=pltpu.VMEM)
    dma = pltpu.SemaphoreType.DMA
    return pl.pallas_call(
        kernel,
        out_shape=jax.ShapeDtypeStruct((1, B, R), F32),
        in_specs=[hbm, hbm, hbm, hbm, vmem, pl.BlockSpec(memory_space=pltpu.SMEM)],
        out_specs=vmem,
        scratch_shapes=[
            pltpu.VMEM((NX, NZ, B, R), BF16),
            pltpu.VMEM((NX, NZ, B, R), BF16),
            pltpu.VMEM((TOK, D), BF16),
            pltpu.VMEM((TOK, D), BF16),
            pltpu.VMEM((TOK, D), BF16),
            pltpu.VMEM((TOK, D), BF16),
            pltpu.VMEM((NS, 16, D), BF16),
            pltpu.VMEM((NS, 2, NX, NZ, 8, R), BF16),
            pltpu.VMEM((NS, TOK, 2 * R + 128), BF16),
            pltpu.VMEM((TOK, R), F32),
            pltpu.VMEM((TOK, R), F32),
            pltpu.VMEM((TOK, 128), F32),
            pltpu.VMEM((TOK, R), BF16),
            pltpu.VMEM((TOK, R), F32),
            pltpu.VMEM((TOK, 128), F32),
            pltpu.VMEM((TOK, R), BF16),
            pltpu.VMEM((4 * R, TOK), BF16),
            pltpu.VMEM((NX, NZ, R, B), F32),
            pltpu.VMEM((NX, 2, 4, 128, B), BF16),
            pltpu.VMEM((NX, 2, 4, 128, B), BF16),
            pltpu.VMEM((NZ, 2, 2, 128, B), BF16),
            pltpu.VMEM((NZ, 2, 2, 128, B), BF16),
            pltpu.VMEM((NX, 128, B), F32),
            pltpu.VMEM((NZ, 128, B), F32),
            pltpu.VMEM((2, 2, 128, B), BF16),
            pltpu.VMEM((2, 2, 128, B), BF16),
            pltpu.VMEM((2, 4, 128, B), BF16),
            pltpu.VMEM((2, 4, 128, B), BF16),
            dma((4,)),
            dma((GATHER_CHANNELS,)),
            dma((GATHER_CHANNELS,)),
            dma((NM,)),
            dma((NS,)),
            dma((RS_CHANNELS,)),
            dma((NM,)),
            dma((NS,)),
            dma((NS,)),
            dma((NS,)),
            dma((NS, 8)),
            dma((NS, 8)),
            dma((NS, 4)),
            dma((NS, 4)),
        ],
        compiler_params=pltpu.CompilerParams(
            collective_id=0, has_side_effects=True, vmem_limit_bytes=62 * 1024 * 1024
        ),
    )(
        tokens,
        cotangent,
        down_weight[0],
        up_weight[0],
        norm_gain,
        lengths,
    )


def solution(mesh):
    split = Mesh(mesh.devices.reshape(NS, NX, NZ), ("section", "x", "z"))
    dp = ("x", "z")
    return jax.shard_map(
        per_device,
        mesh=split,
        in_specs=(
            P(dp, None),
            P(dp, None),
            P("section", dp, None),
            P("section", dp, None),
            P("section", None),
            P(dp, None),
        ),
        out_specs=P("section", dp, None),
        check_vma=False,
    )
```

```python
import functools

import jax
import jax.numpy as jnp
from jax import lax
from jax.experimental import pallas as pl
from jax.experimental.pallas import tpu as pltpu
from jax.sharding import Mesh
from jax.sharding import PartitionSpec as P

MESH = pl.DeviceIdType.MESH
F32 = jnp.float32
BF16 = jnp.bfloat16
NX, NZ, NS = 4, 8, 8
B = 256
D = 8192
R = 256
TOK = 128
MB = 16
XROWS = 128
NC = 4
PER = NX * NZ // NC
NM = TOK // MB
EPS = 1e-05

GATHER_CHANNELS = 76
RS_CHANNELS = 76


CUT = 304


def half_z(d):
    return pl.ds(0, 160) if d > 0 else pl.ds(160, CUT - 160)


def half_x(d):
    return pl.ds(CUT, 112) if d > 0 else pl.ds(CUT + 112, 96)


ZFIRST, XFIRST = pl.ds(0, CUT), pl.ds(CUT, 2 * B - CUT)


def kernel(
    tok, cot, dwn, upw, gain, lens, out,
    w, hbuf, hout, nbuf, cbuf, ebuf, mat, msg, gacc, hup, csum, actbuf, prebuf, invbuf, pgbuf, masked, fsum,
    rb_s, rb_r, ra_s, ra_r, gb, ga, sb_s, sb_r, sa_s, sa_r,
    lsem, ssem, grecv, frecv, brecv, rrecv, psem, bsend, esend, erecv, hsend, zsend, zrecv, xsend, xrecv,
):
    s = lax.axis_index("section")
    x = lax.axis_index("x")
    z = lax.axis_index("z")

    def xo(k):
        return lax.rem(x + k + NX, NX)

    def zo(k):
        return lax.rem(z + k + NZ, NZ)

    own = (
        pltpu.make_async_copy(dwn, w.at[x, z, pl.ds(B, B)], lsem.at[0]),
        pltpu.make_async_copy(upw, w.at[x, z, pl.ds(0, B)], lsem.at[1]),
    )
    for c in own:
        c.start()

    barrier = pltpu.get_barrier_semaphore()
    s_next, s_prev = lax.rem(s + 1, NS), lax.rem(s + NS - 1, NS)
    for where in (
        {"x": xo(1)}, {"x": xo(-1)}, {"z": zo(1)}, {"z": zo(-1)},
        *({"section": lax.rem(s + k, NS)} for k in range(1, NS)),
    ):
        pl.semaphore_signal(barrier, inc=1, device_id=where, device_id_type=MESH)
    pl.semaphore_wait(barrier, 3 + NS)

    for c in own:
        c.wait()

    first = pltpu.make_async_copy(tok, hbuf, lsem.at[2])
    cotangent = pltpu.make_async_copy(cot, cbuf, lsem.at[3])
    cotangent.start()

    def clear(j, carry):
        ebuf[j] = jnp.zeros((16, D), BF16)
        return carry

    lax.fori_loop(0, s + 1, clear, 0)

    @pl.when(s == 0)
    def _():
        first.start()

    sent = []
    counter = [0]
    chan = {}

    def number(key):
        if key not in chan:
            chan[key] = counter[0]
            counter[0] += 1
        return chan[key]

    def hop(axis, d):
        return {"x": xo(d)} if axis == "x" else {"z": zo(d)}

    def g_send(key, block, axis, d):
        k = number(key)
        c = pltpu.make_async_remote_copy(
            src_ref=block, dst_ref=block, send_sem=ssem.at[k], recv_sem=grecv.at[k],
            device_id=hop(axis, d), device_id_type=MESH,
        )
        c.start()
        sent.append(c)

    def g_wait(key, block, axis, d):
        k = number(key)
        pltpu.make_async_remote_copy(
            src_ref=block, dst_ref=block, send_sem=ssem.at[k], recv_sem=grecv.at[k],
            device_id=hop(axis, d), device_id_type=MESH,
        ).wait_recv()

    XOFF = (0, -1, 1, 2)
    ZOFF = (0, -1, 1, -2, 2, -3, 3, 4)

    def send_dx():
        for d in (1, -1):
            g_send(("dX", d), w.at[x, z, XFIRST], "x", d)

    def wait_dx():
        for d in (1, -1):
            g_wait(("dX", d), w.at[xo(-d), z, XFIRST], "x", d)

    def send_dx2():
        for d in (1, -1):
            g_send(("dX2", d), w.at[xo(-d), z, half_x(d)], "x", d)

    def wait_dx2():
        for d in (1, -1):
            g_wait(("dX2", d), w.at[xo(2), z, half_x(d)], "x", d)

    def send_uz(j):
        for d in (1, -1):
            rows = ZFIRST if j < 4 else half_z(d)
            g_send(("uZ", d, j), w.at[x, zo(-d * (j - 1)), rows], "z", d)

    def wait_uz(j):
        for d in (1, -1):
            rows = ZFIRST if j < 4 else half_z(d)
            g_wait(("uZ", d, j), w.at[x, zo(-d * j), rows], "z", d)

    def send_dz(j, c):
        for d in (1, -1):
            rows = XFIRST if j < 4 else half_x(d)
            g_send(("dZ", d, j, c), w.at[xo(XOFF[c]), zo(-d * (j - 1)), rows], "z", d)

    def wait_dz(j, c):
        for d in (1, -1):
            rows = XFIRST if j < 4 else half_x(d)
            g_wait(("dZ", d, j, c), w.at[xo(XOFF[c]), zo(-d * j), rows], "z", d)

    def send_ux(q):
        for d in (1, -1):
            g_send(("uX", d, q), w.at[x, zo(ZOFF[q]), ZFIRST], "x", d)

    def wait_ux(q):
        for d in (1, -1):
            g_wait(("uX", d, q), w.at[xo(-d), zo(ZOFF[q]), ZFIRST], "x", d)

    def send_ux2(q):
        for d in (1, -1):
            g_send(("uX2", d, q), w.at[xo(-d), zo(ZOFF[q]), half_z(d)], "x", d)

    def wait_ux2(q):
        for d in (1, -1):
            g_wait(("uX2", d, q), w.at[xo(2), zo(ZOFF[q]), half_z(d)], "x", d)

    def relay_ux(q):
        wait_ux(q)
        send_ux2(q)

    def relay_dz(j, c):
        wait_dz(j, c)
        send_dz(j + 1, c)

    send_dx()
    send_uz(1)
    send_dz(1, 0)
    send_ux(0)
    wait_dx()
    send_dx2()
    send_dz(1, 1)
    send_dz(1, 2)
    wait_uz(1)
    send_uz(2)
    send_ux(1)
    send_ux(2)
    wait_dx2()
    send_dz(1, 3)
    relay_ux(0)
    relay_dz(1, 0)
    wait_uz(2)
    send_uz(3)
    send_ux(3)
    send_ux(4)
    relay_ux(1)
    relay_ux(2)
    relay_dz(1, 1)
    relay_dz(1, 2)
    wait_uz(3)
    send_uz(4)
    send_ux(5)
    send_ux(6)
    relay_dz(1, 3)
    relay_dz(2, 0)
    relay_ux(3)
    relay_ux(4)
    relay_dz(2, 1)
    relay_dz(2, 2)
    wait_uz(4)
    send_ux(7)
    relay_dz(2, 3)
    relay_ux(5)
    relay_ux(6)
    for c in range(4):
        relay_dz(3, c)
    relay_ux(7)
    for c in range(4):
        wait_dz(4, c)
    for q in range(8):
        wait_ux2(q)
    for c in sent:
        c.wait_send()
    sent.clear()

    @pl.when(s == 0)
    def _():
        first.wait()

    LATE = 4
    begin_at = jnp.where(s >= 5, -1, jnp.where(s == 4, 1, jnp.where(s == 3, 5, jnp.where(s == 2, 6, NM))))
    hand_at = jnp.where(s >= 5, -1, jnp.where(s == 3, 4, NM - 1))

    def blk(r):
        return slice(r * B, (r + 1) * B)

    replica = x * NZ + z
    odd = lax.rem(s, 2)

    def e_copy(j, below):
        return pltpu.make_async_remote_copy(
            src_ref=ebuf.at[j], dst_ref=ebuf.at[j], send_sem=esend.at[below], recv_sem=erecv.at[j],
            device_id={"section": below}, device_id_type=MESH,
        )

    @pl.when(s > 0)
    def _():
        pick = lax.broadcasted_iota(jnp.int32, (8, R), 1) == (
            lax.broadcasted_iota(jnp.int32, (8, R), 0) + replica * 8
        )
        pick = jnp.where(pick, 1.0, 0.0).astype(BF16)
        for r in range(NX * NZ):
            rows_d = lax.dot_general(
                pick, w[r // NZ, r % NZ, B : 2 * B], (((1,), (1,)), ((), ())), preferred_element_type=F32
            )
            rows_u = lax.dot_general(
                pick, w[r // NZ, r % NZ, 0:B], (((1,), (1,)), ((), ())), preferred_element_type=F32
            )
            ebuf[s, :, blk(r)] = jnp.concatenate([rows_d * gain[:, blk(r)], rows_u], axis=0).astype(BF16)

        @pl.when(odd == 1)
        def _():
            e_copy(s, s - 1).start()

        def offer(t, carry):
            e_copy(s, s - 1 - odd - 2 * t).start()
            return carry

        lax.fori_loop(0, s // 2, offer, 0)

    def z_copy(j, h, d, arriving):
        k = zo(-d * h) if arriving else zo(-d * (h - 1))
        e = 0 if d > 0 else 1
        ref = mat.at[j, :, x, k] if h < 4 else mat.at[j, e, x, k]
        return pltpu.make_async_remote_copy(
            src_ref=ref, dst_ref=ref, send_sem=zsend.at[j, 2 * h - 2 + e], recv_sem=zrecv.at[j, 2 * h - 2 + e],
            device_id={"z": zo(d)}, device_id_type=MESH,
        )

    def x_copy(j, h, d, arriving):
        k = xo(-d * h) if arriving else xo(-d * (h - 1))
        e = 0 if d > 0 else 1
        ref = mat.at[j, :, k] if h < 2 else mat.at[j, e, k]
        return pltpu.make_async_remote_copy(
            src_ref=ref, dst_ref=ref, send_sem=xsend.at[j, 2 * h - 2 + e], recv_sem=xrecv.at[j, 2 * h - 2 + e],
            device_id={"x": xo(d)}, device_id_type=MESH,
        )

    def above(body):
        def step(t, carry):
            body(s + 1 + t)
            return carry

        lax.fori_loop(0, NS - 1 - s, step, 0)

    def hand_on():
        def one(j):
            e_copy(j, s_prev).wait_recv()
            pltpu.make_async_remote_copy(
                src_ref=ebuf.at[j], dst_ref=ebuf.at[j], send_sem=hsend.at[j], recv_sem=erecv.at[j],
                device_id={"section": s_prev}, device_id_type=MESH,
            ).start()

        above(one)

    def handed():
        above(lambda j: pltpu.make_async_remote_copy(
            src_ref=ebuf.at[j], dst_ref=ebuf.at[j], send_sem=hsend.at[j], recv_sem=erecv.at[j],
            device_id={"section": s_prev}, device_id_type=MESH,
        ).wait_send())

    def exchange_begin():
        @pl.when(odd == 0)
        def _():
            above(lambda j: e_copy(j, s_prev).wait_recv())

        acc = jnp.zeros((NS * 16, R), F32)
        for r in range(NX * NZ):
            rows_e = ebuf[:, :, blk(r)].reshape(NS * 16, B)
            acc = acc + jnp.dot(rows_e, w[r // NZ, r % NZ, 0:B], preferred_element_type=F32)
        for j in range(1, NS):
            mat[j, 0, x, z] = acc[16 * j : 16 * j + 8].astype(BF16)
            mat[j, 1, x, z] = acc[16 * j + 8 : 16 * j + 16].astype(BF16)

        def begin(j):
            for d in (1, -1):
                z_copy(j, 1, d, False).start()

        above(begin)

    def along(h):
        def on(j):
            for d in (1, -1):
                z_copy(j, h, d, True).wait_recv()
            for d in (1, -1):
                z_copy(j, h + 1, d, False).start()

        above(on)

    def turn():
        def one(j):
            for d in (1, -1):
                z_copy(j, 4, d, True).wait_recv()
            for d in (1, -1):
                x_copy(j, 1, d, False).start()

        above(one)

    def across():
        def one(j):
            for d in (1, -1):
                x_copy(j, 1, d, True).wait_recv()
            for d in (1, -1):
                x_copy(j, 2, d, False).start()

        above(one)

    def finish():
        def one(j):
            for d in (1, -1):
                x_copy(j, 2, d, True).wait_recv()

        above(one)

    exchange_steps = (
        lambda: along(1), lambda: along(2), lambda: along(3), turn, across, finish,
    )

    def exchange_sent():
        def one(j):
            for d in (1, -1):
                for h in (1, 2, 3, 4):
                    z_copy(j, h, d, False).wait_send()
                for h in (1, 2):
                    x_copy(j, h, d, False).wait_send()

        above(one)

    def start_gradient():
        cotangent.wait()
        acc = jnp.zeros((TOK, R), F32)
        for r in range(NX * NZ):
            acc = acc + jnp.dot(cbuf[:, blk(r)], w[r // NZ, r % NZ, 0:B], preferred_element_type=F32)
        gacc[...] = acc

    @pl.when(s >= LATE)
    def _():
        start_gradient()

    @pl.when((odd == 1) & (hand_at < 0))
    def _():
        hand_on()

    @pl.when((begin_at < 0) & (s < NS - 1))
    def _():
        exchange_begin()

    def micro(i):
        return pl.ds(pl.multiple_of(i * MB, MB), MB)

    def f_copy(i, q):
        cols = pl.ds(q * PER * B, PER * B)
        return pltpu.make_async_remote_copy(
            src_ref=hout.at[micro(i), cols], dst_ref=hbuf.at[micro(i), cols],
            send_sem=psem.at[i, q], recv_sem=frecv.at[i, q],
            device_id={"section": s_next}, device_id_type=MESH,
        )

    def forward(i, carry):
        rows = micro(i)
        squares = jnp.zeros((MB, B), F32)
        accs = [jnp.zeros((MB, 128), F32)] * 2
        for q in range(NC):
            @pl.when(s > 0)
            def _(q=q):
                f_copy(i, q).wait_recv()

            for r in range(q * PER, (q + 1) * PER):
                h = hbuf[rows, blk(r)].astype(F32)
                squares = squares + h * h
                n = (h * gain[:, blk(r)]).astype(BF16)
                nbuf[rows, blk(r)] = n
                for e in range(2):
                    cut = w[r // NZ, r % NZ, B : 2 * B, e * 128 : (e + 1) * 128]
                    accs[e] = accs[e] + jnp.dot(n, cut, preferred_element_type=F32)
        inv = lax.rsqrt(jnp.sum(squares, axis=-1, keepdims=True) * (1.0 / D) + EPS)
        acc = jnp.concatenate(accs, axis=1) * inv
        prebuf[rows, :] = acc
        invbuf[rows, :] = jnp.broadcast_to(inv, (MB, 128))
        act = (acc * jax.nn.sigmoid(acc)).astype(BF16)
        actbuf[rows, :] = act

        @pl.when(s < NS - 1)
        def _():
            for q in range(NC):
                for r in range(q * PER, (q + 1) * PER):
                    up = lax.dot_general(
                        act, w[r // NZ, r % NZ, 0:B], (((1,), (1,)), ((), ())), preferred_element_type=F32
                    )
                    hout[rows, blk(r)] = (hbuf[rows, blk(r)].astype(F32) + up).astype(BF16)
                f_copy(i, q).start()

        @pl.when((odd == 1) & (i == hand_at))
        def _():
            hand_on()

        @pl.when(s < NS - 1)
        def _():
            pl.when(i == begin_at)(exchange_begin)
            for k, step in enumerate(exchange_steps):
                pl.when(i == begin_at + 1 + k)(step)

        return carry

    lax.fori_loop(0, NM, forward, 0)

    @pl.when(begin_at >= NM)
    def _():
        exchange_begin()

    @pl.when(s < LATE)
    def _():
        start_gradient()

    @pl.when(s < NS - 1)
    def _():
        acc = jnp.zeros((TOK, R), F32)
        for r in range(NX * NZ):
            acc = acc + jnp.dot(hout[:, blk(r)], w[r // NZ, r % NZ, 0:B], preferred_element_type=F32)
        hup[...] = acc
        for k, step in enumerate(exchange_steps):
            pl.when(begin_at + 1 + k >= NM)(step)

    csum[...] = jnp.zeros((TOK, 128), F32)

    HT = TOK // 2

    def b_copy(j, u):
        part = msg.at[j, pl.ds(u * HT, HT)]
        return pltpu.make_async_remote_copy(
            src_ref=part, dst_ref=part, send_sem=bsend.at[j, u], recv_sem=brecv.at[j, u],
            device_id={"section": s_prev}, device_id_type=MESH,
        )

    def receive(j, u):
        b_copy(j, u).wait_recv()

        @pl.when(s > 0)
        def _():
            b_copy(j, u).start()

    def accumulate(j, rows):
        c = msg[j, rows, 2 * R : 2 * R + 128].astype(F32)
        csum[rows, :] += c
        from_down = jnp.dot(
            msg[j, rows, 0:R], mat[j, 0].reshape(R, R), preferred_element_type=F32
        )
        from_up = jnp.dot(
            msg[j, rows, R : 2 * R], mat[j, 1].reshape(R, R), preferred_element_type=F32
        )
        both = jnp.concatenate([c, c], axis=1)
        gacc[rows, :] += from_down + from_up - both * hup[rows, :]

    def arrive(t, carry):
        j = NS - 1 - t
        for u in (0, 1):
            receive(j, u)
        accumulate(j, slice(0, TOK))
        return carry

    lax.fori_loop(0, NS - 2 - s, arrive, 0)

    for u in (0, 1):
        rows = slice(u * HT, (u + 1) * HT)

        @pl.when(s < NS - 1)
        def _(u=u, rows=rows):
            receive(s + 1, u)
            accumulate(s + 1, rows)

        pre = prebuf[rows, :]
        sig = jax.nn.sigmoid(pre)
        inv = invbuf[rows, 0:1]
        wide = gacc[rows, :] * sig * (1.0 + pre * (1.0 - sig))
        scaled = (wide * inv).astype(BF16)
        pgbuf[rows, :] = scaled

        @pl.when(s > 0)
        def _(u=u, rows=rows, pre=pre, inv=inv, wide=wide, scaled=scaled):
            coef = inv * inv * (jnp.sum(wide * pre, axis=-1, keepdims=True) * (1.0 / D))
            msg[s, rows, 0:R] = scaled
            msg[s, rows, R : 2 * R] = (actbuf[rows, :].astype(F32) * (-csum[rows, 0:1])).astype(BF16)
            msg[s, rows, 2 * R : 2 * R + 128] = jnp.broadcast_to(coef, (HT, 128)).astype(BF16)
            b_copy(s, u).start()

    pgt = pgbuf[...].astype(F32).T
    position = lax.broadcasted_iota(jnp.int32, (1, TOK), 1)
    start = jnp.int32(0)
    for j in range(4):
        end = start + lens[0, j]
        inside = (position >= start) & (position < end)
        masked[j * R : (j + 1) * R, :] = jnp.where(inside, pgt, 0.0).astype(BF16)
        start = end

    def square(count, where):
        def one(t, carry):
            a, b = where(t)
            cols = pl.ds(pl.multiple_of((a * NZ + b) * B, B), B)
            p = jnp.dot(masked[...], nbuf[:, cols], preferred_element_type=F32)
            p = p * p
            fsum[a, b] = (p[0:R] + p[R : 2 * R]) + (p[2 * R : 3 * R] + p[3 * R : 4 * R])
            return carry

        lax.fori_loop(0, count, one, 0)

    rcount = [0]
    rchan = {}

    def rnumber(key):
        if key not in rchan:
            rchan[key] = rcount[0]
            rcount[0] += 1
        return rchan[key]

    def r_copy(key, src, dst, axis, d):
        k = rnumber(key)
        return pltpu.make_async_remote_copy(
            src_ref=src, dst_ref=dst, send_sem=ssem.at[k], recv_sem=rrecv.at[k],
            device_id=hop(axis, d), device_id_type=MESH,
        )

    def go(c):
        c.start()
        sent.append(c)

    def side(d):
        return 0 if d > 0 else 1


    def ring(key, axis, depth, mine, sbuf, rbuf, d, j):
        e = side(d)
        value = mine(j * d)
        m = value.shape[0] // 2
        part = slice(0, m) if d > 0 else slice(m, 2 * m)
        HALF, FULL = pl.ds(0, m), pl.ds(0, 2 * m)
        span = HALF if j == depth else FULL
        if j == depth:
            sbuf[e, j - 1, 0:m] = value[part].astype(BF16)
        else:
            if j == depth - 1:
                r_copy(key + (d, j + 1), sbuf.at[e, j, HALF], rbuf.at[e, j, HALF], axis, d).wait_recv()
                got = rbuf[e, j, 0:m].astype(F32)
                keep = slice(m - part.start, 2 * m - part.start)
                sbuf[e, j - 1, part] = (value[part] + got).astype(BF16)
                sbuf[e, j - 1, keep] = value[keep].astype(BF16)
            else:
                r_copy(key + (d, j + 1), sbuf.at[e, j, FULL], rbuf.at[e, j, FULL], axis, d).wait_recv()
                sbuf[e, j - 1] = (value + rbuf[e, j].astype(F32)).astype(BF16)
        go(r_copy(key + (d, j), sbuf.at[e, j - 1, span], rbuf.at[e, j - 1, span], axis, d))

    def ring_end(key, axis, mine, sbuf, rbuf):
        value = mine(0)
        FULL = pl.ds(0, value.shape[0])
        for d in (1, -1):
            e = side(d)
            r_copy(key + (d, 1), sbuf.at[e, 0, FULL], rbuf.at[e, 0, FULL], axis, d).wait_recv()
            value = value + rbuf[e, 0].astype(F32)
        return value

    def stage_a(q, d, j):
        ring(("A1", q), "x", 2, lambda k: fsum[xo(k), q, 0:XROWS], ra_s.at[q], ra_r.at[q], d, j)

    def stage_b(c, d, j):
        ring(("B1", c), "z", 4, lambda k: fsum[c, zo(k), XROWS:R], rb_s.at[c], rb_r.at[c], d, j)

    square(4, lambda t: (t, zo(4)))
    for c in range(NX):
        for d in (1, -1):
            stage_b(c, d, 4)
    square(7, lambda t: (xo(2), zo(5 + t)))
    for q in range(NZ):
        for d in (1, -1):
            stage_a(q, d, 2)
    square(6, lambda t: (xo(3 + lax.rem(t, 3)), zo(3 + 2 * (t // 3))))
    for c in range(NX):
        for d in (1, -1):
            stage_b(c, d, 3)
    square(10, lambda t: (xo(1 + 2 * (t // 5)), zo(6 + lax.rem(t, 5))))
    for q in range(NZ):
        for d in (1, -1):
            stage_a(q, d, 1)
    square(5, lambda t: (x, zo(6 + t)))
    for c in range(NX):
        for d in (1, -1):
            stage_b(c, d, 2)
    for c in range(NX):
        for d in (1, -1):
            stage_b(c, d, 1)
    for q in range(NZ):
        ga[q] = ring_end(("A1", q), "x", lambda k: fsum[xo(k), q, 0:XROWS], ra_s.at[q], ra_r.at[q])

    def last_a(d, j):
        ring(("A2",), "z", 4, lambda k: ga[zo(k)], sa_s, sa_r, d, j)

    def last_b(d, j):
        ring(("B2",), "x", 2, lambda k: gb[xo(k)], sb_s, sb_r, d, j)

    for d in (1, -1):
        last_a(d, 4)
    for c in range(NX):
        gb[c] = ring_end(("B1", c), "z", lambda k: fsum[c, zo(k), XROWS:R], rb_s.at[c], rb_r.at[c])
    for d in (1, -1):
        last_b(d, 2)
    for d in (1, -1):
        last_a(d, 3)
    for d in (1, -1):
        last_b(d, 1)
    for j in (2, 1):
        for d in (1, -1):
            last_a(d, j)
    low = ring_end(("A2",), "z", lambda k: ga[zo(k)], sa_s, sa_r)
    high = ring_end(("B2",), "x", lambda k: gb[xo(k)], sb_s, sb_r)
    scale = 1.0 / (TOK * NX * NZ)
    out[0] = jnp.concatenate([low, high], axis=0).T * scale
    for c in sent:
        c.wait_send()

    exchange_sent()

    @pl.when(s < NS - 1)
    def _():
        @pl.loop(0, NM)
        def _(i):
            for q in range(NC):
                f_copy(i, q).wait_send()

    @pl.when(s > 0)
    def _():
        def done(t, carry):
            for u in (0, 1):
                b_copy(s + t, u).wait_send()
            return carry

        lax.fori_loop(0, NS - s, done, 0)

        @pl.when(odd == 1)
        def _():
            e_copy(s, s - 1).wait_send()

        def offered(t, carry):
            e_copy(s, s - 1 - odd - 2 * t).wait_send()
            return carry

        lax.fori_loop(0, s // 2, offered, 0)

    @pl.when(odd == 1)
    def _():
        handed()


def per_device(tokens, cotangent, down_weight, up_weight, norm_gain, lengths):
    hbm = pl.BlockSpec(memory_space=pl.ANY)
    vmem = pl.BlockSpec(memory_space=pltpu.VMEM)
    dma = pltpu.SemaphoreType.DMA
    return pl.pallas_call(
        kernel,
        out_shape=jax.ShapeDtypeStruct((1, B, R), F32),
        in_specs=[hbm, hbm, hbm, hbm, vmem, pl.BlockSpec(memory_space=pltpu.SMEM)],
        out_specs=vmem,
        scratch_shapes=[
            pltpu.VMEM((NX, NZ, 2 * B, R), BF16),
            pltpu.VMEM((TOK, D), BF16),
            pltpu.VMEM((TOK, D), BF16),
            pltpu.VMEM((TOK, D), BF16),
            pltpu.VMEM((TOK, D), BF16),
            pltpu.VMEM((NS, 16, D), BF16),
            pltpu.VMEM((NS, 2, NX, NZ, 8, R), BF16),
            pltpu.VMEM((NS, TOK, 2 * R + 128), BF16),
            pltpu.VMEM((TOK, R), F32),
            pltpu.VMEM((TOK, R), F32),
            pltpu.VMEM((TOK, 128), F32),
            pltpu.VMEM((TOK, R), BF16),
            pltpu.VMEM((TOK, R), F32),
            pltpu.VMEM((TOK, 128), F32),
            pltpu.VMEM((TOK, R), BF16),
            pltpu.VMEM((4 * R, TOK), BF16),
            pltpu.VMEM((NX, NZ, R, B), F32),
            pltpu.VMEM((NX, 2, 4, R - XROWS, B), BF16),
            pltpu.VMEM((NX, 2, 4, R - XROWS, B), BF16),
            pltpu.VMEM((NZ, 2, 2, XROWS, B), BF16),
            pltpu.VMEM((NZ, 2, 2, XROWS, B), BF16),
            pltpu.VMEM((NX, R - XROWS, B), F32),
            pltpu.VMEM((NZ, XROWS, B), F32),
            pltpu.VMEM((2, 2, R - XROWS, B), BF16),
            pltpu.VMEM((2, 2, R - XROWS, B), BF16),
            pltpu.VMEM((2, 4, XROWS, B), BF16),
            pltpu.VMEM((2, 4, XROWS, B), BF16),
            dma((4,)),
            dma((GATHER_CHANNELS,)),
            dma((GATHER_CHANNELS,)),
            dma((NM, NC)),
            dma((NS, 2)),
            dma((RS_CHANNELS,)),
            dma((NM, NC)),
            dma((NS, 2)),
            dma((NS,)),
            dma((NS,)),
            dma((NS,)),
            dma((NS, 8)),
            dma((NS, 8)),
            dma((NS, 4)),
            dma((NS, 4)),
        ],
        compiler_params=pltpu.CompilerParams(
            collective_id=0, has_side_effects=True, vmem_limit_bytes=62 * 1024 * 1024
        ),
    )(
        tokens,
        cotangent,
        down_weight[0],
        up_weight[0],
        norm_gain,
        lengths,
    )


def solution(mesh):
    split = Mesh(mesh.devices.reshape(NS, NX, NZ), ("section", "x", "z"))
    dp = ("x", "z")
    return jax.shard_map(
        per_device,
        mesh=split,
        in_specs=(
            P(dp, None),
            P(dp, None),
            P("section", dp, None),
            P("section", dp, None),
            P("section", None),
            P(dp, None),
        ),
        out_specs=P("section", dp, None),
        check_vma=False,
    )
```

```python
import functools

import jax
import jax.numpy as jnp
from jax import lax
from jax.experimental import pallas as pl
from jax.experimental.pallas import tpu as pltpu
from jax.sharding import Mesh
from jax.sharding import PartitionSpec as P

MESH = pl.DeviceIdType.MESH
F32 = jnp.float32
BF16 = jnp.bfloat16
NX, NZ, NS = 4, 8, 8
B = 256
D = 8192
R = 256
TOK = 128
MB = 16
XROWS = 128
NC = 4
PER = NX * NZ // NC
NM = TOK // MB
EPS = 1e-05

GATHER_CHANNELS = 76
RS_CHANNELS = 76


CUT = 304


def half_z(d):
    return pl.ds(0, 160) if d > 0 else pl.ds(160, CUT - 160)


def half_x(d):
    return pl.ds(CUT, 112) if d > 0 else pl.ds(CUT + 112, 96)


ZFIRST, XFIRST = pl.ds(0, CUT), pl.ds(CUT, 2 * B - CUT)


def kernel(
    tok, cot, dwn, upw, gain, lens, out,
    w, hbuf, hout, nbuf, cbuf, ebuf, mat, msg, gacc, hup, csum, actbuf, prebuf, invbuf, pgbuf, masked, fsum,
    rb_s, rb_r, ra_s, ra_r, gb, ga, sb_s, sb_r, sa_s, sa_r,
    lsem, ssem, grecv, frecv, brecv, rrecv, psem, bsend, esend, erecv, hsend, zsend, zrecv, xsend, xrecv,
):
    s = lax.axis_index("section")
    x = lax.axis_index("x")
    z = lax.axis_index("z")

    def xo(k):
        return lax.rem(x + k + NX, NX)

    def zo(k):
        return lax.rem(z + k + NZ, NZ)

    own = (
        pltpu.make_async_copy(dwn, w.at[x, z, pl.ds(B, B)], lsem.at[0]),
        pltpu.make_async_copy(upw, w.at[x, z, pl.ds(0, B)], lsem.at[1]),
    )
    for c in own:
        c.start()

    barrier = pltpu.get_barrier_semaphore()
    s_next, s_prev = lax.rem(s + 1, NS), lax.rem(s + NS - 1, NS)
    for where in (
        {"x": xo(1)}, {"x": xo(-1)}, {"z": zo(1)}, {"z": zo(-1)},
        *({"section": lax.rem(s + k, NS)} for k in range(1, NS)),
    ):
        pl.semaphore_signal(barrier, inc=1, device_id=where, device_id_type=MESH)
    pl.semaphore_wait(barrier, 3 + NS)

    for c in own:
        c.wait()

    first = pltpu.make_async_copy(tok, hbuf, lsem.at[2])
    cotangent = pltpu.make_async_copy(cot, cbuf, lsem.at[3])
    cotangent.start()

    def clear(j, carry):
        ebuf[j] = jnp.zeros((16, D), BF16)
        return carry

    lax.fori_loop(0, s + 1, clear, 0)

    @pl.when(s == 0)
    def _():
        first.start()

    sent = []
    counter = [0]
    chan = {}

    def number(key):
        if key not in chan:
            chan[key] = counter[0]
            counter[0] += 1
        return chan[key]

    def hop(axis, d):
        return {"x": xo(d)} if axis == "x" else {"z": zo(d)}

    def g_send(key, block, axis, d):
        k = number(key)
        c = pltpu.make_async_remote_copy(
            src_ref=block, dst_ref=block, send_sem=ssem.at[k], recv_sem=grecv.at[k],
            device_id=hop(axis, d), device_id_type=MESH,
        )
        c.start()
        sent.append(c)

    def g_wait(key, block, axis, d):
        k = number(key)
        pltpu.make_async_remote_copy(
            src_ref=block, dst_ref=block, send_sem=ssem.at[k], recv_sem=grecv.at[k],
            device_id=hop(axis, d), device_id_type=MESH,
        ).wait_recv()

    XOFF = (0, -1, 1, 2)
    ZOFF = (0, -1, 1, -2, 2, -3, 3, 4)

    def send_dx():
        for d in (1, -1):
            g_send(("dX", d), w.at[x, z, XFIRST], "x", d)

    def wait_dx():
        for d in (1, -1):
            g_wait(("dX", d), w.at[xo(-d), z, XFIRST], "x", d)

    def send_dx2():
        for d in (1, -1):
            g_send(("dX2", d), w.at[xo(-d), z, half_x(d)], "x", d)

    def wait_dx2():
        for d in (1, -1):
            g_wait(("dX2", d), w.at[xo(2), z, half_x(d)], "x", d)

    def send_uz(j):
        for d in (1, -1):
            rows = ZFIRST if j < 4 else half_z(d)
            g_send(("uZ", d, j), w.at[x, zo(-d * (j - 1)), rows], "z", d)

    def wait_uz(j):
        for d in (1, -1):
            rows = ZFIRST if j < 4 else half_z(d)
            g_wait(("uZ", d, j), w.at[x, zo(-d * j), rows], "z", d)

    def send_dz(j, c):
        for d in (1, -1):
            rows = XFIRST if j < 4 else half_x(d)
            g_send(("dZ", d, j, c), w.at[xo(XOFF[c]), zo(-d * (j - 1)), rows], "z", d)

    def wait_dz(j, c):
        for d in (1, -1):
            rows = XFIRST if j < 4 else half_x(d)
            g_wait(("dZ", d, j, c), w.at[xo(XOFF[c]), zo(-d * j), rows], "z", d)

    def send_ux(q):
        for d in (1, -1):
            g_send(("uX", d, q), w.at[x, zo(ZOFF[q]), ZFIRST], "x", d)

    def wait_ux(q):
        for d in (1, -1):
            g_wait(("uX", d, q), w.at[xo(-d), zo(ZOFF[q]), ZFIRST], "x", d)

    def send_ux2(q):
        for d in (1, -1):
            g_send(("uX2", d, q), w.at[xo(-d), zo(ZOFF[q]), half_z(d)], "x", d)

    def wait_ux2(q):
        for d in (1, -1):
            g_wait(("uX2", d, q), w.at[xo(2), zo(ZOFF[q]), half_z(d)], "x", d)

    def relay_ux(q):
        wait_ux(q)
        send_ux2(q)

    def relay_dz(j, c):
        wait_dz(j, c)
        send_dz(j + 1, c)

    send_dx()
    send_uz(1)
    send_dz(1, 0)
    send_ux(0)
    wait_dx()
    send_dx2()
    send_dz(1, 1)
    send_dz(1, 2)
    wait_uz(1)
    send_uz(2)
    send_ux(1)
    send_ux(2)
    wait_dx2()
    send_dz(1, 3)
    relay_ux(0)
    relay_dz(1, 0)
    wait_uz(2)
    send_uz(3)
    send_ux(3)
    send_ux(4)
    relay_ux(1)
    relay_ux(2)
    relay_dz(1, 1)
    relay_dz(1, 2)
    wait_uz(3)
    send_uz(4)
    send_ux(5)
    send_ux(6)
    relay_dz(1, 3)
    relay_dz(2, 0)
    relay_ux(3)
    relay_ux(4)
    relay_dz(2, 1)
    relay_dz(2, 2)
    wait_uz(4)
    send_ux(7)
    relay_dz(2, 3)
    relay_ux(5)
    relay_ux(6)
    for c in range(4):
        relay_dz(3, c)
    relay_ux(7)
    for c in range(4):
        wait_dz(4, c)
    for q in range(8):
        wait_ux2(q)
    for c in sent:
        c.wait_send()
    sent.clear()

    @pl.when(s == 0)
    def _():
        first.wait()

    LATE = 4
    begin_at = jnp.where(s >= 5, -1, jnp.where(s == 4, 5, jnp.where(s == 3, 5, jnp.where(s == 2, 6, NM))))
    hand_at = jnp.where(s >= 5, -1, jnp.where(s == 3, 4, NM - 1))

    def blk(r):
        return slice(r * B, (r + 1) * B)

    replica = x * NZ + z
    odd = lax.rem(s, 2)

    def e_copy(j, below):
        return pltpu.make_async_remote_copy(
            src_ref=ebuf.at[j], dst_ref=ebuf.at[j], send_sem=esend.at[below], recv_sem=erecv.at[j],
            device_id={"section": below}, device_id_type=MESH,
        )

    @pl.when(s > 0)
    def _():
        pick = lax.broadcasted_iota(jnp.int32, (8, R), 1) == (
            lax.broadcasted_iota(jnp.int32, (8, R), 0) + replica * 8
        )
        pick = jnp.where(pick, 1.0, 0.0).astype(BF16)
        for r in range(NX * NZ):
            rows_d = lax.dot_general(
                pick, w[r // NZ, r % NZ, B : 2 * B], (((1,), (1,)), ((), ())), preferred_element_type=F32
            )
            rows_u = lax.dot_general(
                pick, w[r // NZ, r % NZ, 0:B], (((1,), (1,)), ((), ())), preferred_element_type=F32
            )
            ebuf[s, :, blk(r)] = jnp.concatenate([rows_d * gain[:, blk(r)], rows_u], axis=0).astype(BF16)

        @pl.when(odd == 1)
        def _():
            e_copy(s, s - 1).start()

        def offer(t, carry):
            e_copy(s, s - 1 - odd - 2 * t).start()
            return carry

        lax.fori_loop(0, s // 2, offer, 0)

    def z_copy(j, h, d, arriving):
        k = zo(-d * h) if arriving else zo(-d * (h - 1))
        e = 0 if d > 0 else 1
        ref = mat.at[j, :, x, k] if h < 4 else mat.at[j, e, x, k]
        return pltpu.make_async_remote_copy(
            src_ref=ref, dst_ref=ref, send_sem=zsend.at[j, 2 * h - 2 + e], recv_sem=zrecv.at[j, 2 * h - 2 + e],
            device_id={"z": zo(d)}, device_id_type=MESH,
        )

    def x_copy(j, h, d, arriving):
        k = xo(-d * h) if arriving else xo(-d * (h - 1))
        e = 0 if d > 0 else 1
        ref = mat.at[j, :, k] if h < 2 else mat.at[j, e, k]
        return pltpu.make_async_remote_copy(
            src_ref=ref, dst_ref=ref, send_sem=xsend.at[j, 2 * h - 2 + e], recv_sem=xrecv.at[j, 2 * h - 2 + e],
            device_id={"x": xo(d)}, device_id_type=MESH,
        )

    def above(body):
        def step(t, carry):
            body(s + 1 + t)
            return carry

        lax.fori_loop(0, NS - 1 - s, step, 0)

    def hand_on():
        def one(j):
            e_copy(j, s_prev).wait_recv()
            pltpu.make_async_remote_copy(
                src_ref=ebuf.at[j], dst_ref=ebuf.at[j], send_sem=hsend.at[j], recv_sem=erecv.at[j],
                device_id={"section": s_prev}, device_id_type=MESH,
            ).start()

        above(one)

    def handed():
        above(lambda j: pltpu.make_async_remote_copy(
            src_ref=ebuf.at[j], dst_ref=ebuf.at[j], send_sem=hsend.at[j], recv_sem=erecv.at[j],
            device_id={"section": s_prev}, device_id_type=MESH,
        ).wait_send())

    def exchange_begin():
        @pl.when(odd == 0)
        def _():
            above(lambda j: e_copy(j, s_prev).wait_recv())

        acc = jnp.zeros((NS * 16, R), F32)
        for r in range(NX * NZ):
            rows_e = ebuf[:, :, blk(r)].reshape(NS * 16, B)
            acc = acc + jnp.dot(rows_e, w[r // NZ, r % NZ, 0:B], preferred_element_type=F32)
        for j in range(1, NS):
            mat[j, 0, x, z] = acc[16 * j : 16 * j + 8].astype(BF16)
            mat[j, 1, x, z] = acc[16 * j + 8 : 16 * j + 16].astype(BF16)

        def begin(j):
            for d in (1, -1):
                z_copy(j, 1, d, False).start()

        above(begin)

    def along(h):
        def on(j):
            for d in (1, -1):
                z_copy(j, h, d, True).wait_recv()
            for d in (1, -1):
                z_copy(j, h + 1, d, False).start()

        above(on)

    def turn():
        def one(j):
            for d in (1, -1):
                z_copy(j, 4, d, True).wait_recv()
            for d in (1, -1):
                x_copy(j, 1, d, False).start()

        above(one)

    def across():
        def one(j):
            for d in (1, -1):
                x_copy(j, 1, d, True).wait_recv()
            for d in (1, -1):
                x_copy(j, 2, d, False).start()

        above(one)

    def finish():
        def one(j):
            for d in (1, -1):
                x_copy(j, 2, d, True).wait_recv()

        above(one)

    exchange_steps = (
        lambda: along(1), lambda: along(2), lambda: along(3), turn, across, finish,
    )

    def exchange_sent():
        def one(j):
            for d in (1, -1):
                for h in (1, 2, 3, 4):
                    z_copy(j, h, d, False).wait_send()
                for h in (1, 2):
                    x_copy(j, h, d, False).wait_send()

        above(one)

    def start_gradient():
        cotangent.wait()
        acc = jnp.zeros((TOK, R), F32)
        for r in range(NX * NZ):
            acc = acc + jnp.dot(cbuf[:, blk(r)], w[r // NZ, r % NZ, 0:B], preferred_element_type=F32)
        gacc[...] = acc

    @pl.when(s >= LATE)
    def _():
        start_gradient()

    @pl.when((odd == 1) & (hand_at < 0))
    def _():
        hand_on()

    @pl.when((begin_at < 0) & (s < NS - 1))
    def _():
        exchange_begin()

    def micro(i):
        return pl.ds(pl.multiple_of(i * MB, MB), MB)

    def f_copy(i, q):
        cols = pl.ds(q * PER * B, PER * B)
        return pltpu.make_async_remote_copy(
            src_ref=hout.at[micro(i), cols], dst_ref=hbuf.at[micro(i), cols],
            send_sem=psem.at[i, q], recv_sem=frecv.at[i, q],
            device_id={"section": s_next}, device_id_type=MESH,
        )

    def forward(i, carry):
        rows = micro(i)
        squares = jnp.zeros((MB, B), F32)
        accs = [jnp.zeros((MB, 128), F32)] * 2
        for q in range(NC):
            @pl.when(s > 0)
            def _(q=q):
                f_copy(i, q).wait_recv()

            for r in range(q * PER, (q + 1) * PER):
                h = hbuf[rows, blk(r)].astype(F32)
                squares = squares + h * h
                n = (h * gain[:, blk(r)]).astype(BF16)
                nbuf[rows, blk(r)] = n
                for e in range(2):
                    cut = w[r // NZ, r % NZ, B : 2 * B, e * 128 : (e + 1) * 128]
                    accs[e] = accs[e] + jnp.dot(n, cut, preferred_element_type=F32)
        inv = lax.rsqrt(jnp.sum(squares, axis=-1, keepdims=True) * (1.0 / D) + EPS)
        acc = jnp.concatenate(accs, axis=1) * inv
        prebuf[rows, :] = acc
        invbuf[rows, :] = jnp.broadcast_to(inv, (MB, 128))
        act = (acc * jax.nn.sigmoid(acc)).astype(BF16)
        actbuf[rows, :] = act

        @pl.when(s < NS - 1)
        def _():
            for q in range(NC):
                for r in range(q * PER, (q + 1) * PER):
                    up = lax.dot_general(
                        act, w[r // NZ, r % NZ, 0:B], (((1,), (1,)), ((), ())), preferred_element_type=F32
                    )
                    hout[rows, blk(r)] = (hbuf[rows, blk(r)].astype(F32) + up).astype(BF16)
                f_copy(i, q).start()

        @pl.when((odd == 1) & (i == hand_at))
        def _():
            hand_on()

        @pl.when(s < NS - 1)
        def _():
            pl.when(i == begin_at)(exchange_begin)
            for k, step in enumerate(exchange_steps):
                pl.when(i == begin_at + 1 + k)(step)

        return carry

    lax.fori_loop(0, NM, forward, 0)

    @pl.when(begin_at >= NM)
    def _():
        exchange_begin()

    @pl.when(s < LATE)
    def _():
        start_gradient()

    @pl.when(s < NS - 1)
    def _():
        acc = jnp.zeros((TOK, R), F32)
        for r in range(NX * NZ):
            acc = acc + jnp.dot(hout[:, blk(r)], w[r // NZ, r % NZ, 0:B], preferred_element_type=F32)
        hup[...] = acc
        for k, step in enumerate(exchange_steps):
            pl.when(begin_at + 1 + k >= NM)(step)

    csum[...] = jnp.zeros((TOK, 128), F32)

    HT = TOK // 2

    def b_copy(j, u):
        part = msg.at[j, pl.ds(u * HT, HT)]
        return pltpu.make_async_remote_copy(
            src_ref=part, dst_ref=part, send_sem=bsend.at[j, u], recv_sem=brecv.at[j, u],
            device_id={"section": s_prev}, device_id_type=MESH,
        )

    def receive(j, u):
        b_copy(j, u).wait_recv()

        @pl.when(s > 0)
        def _():
            b_copy(j, u).start()

    def accumulate(j, rows):
        c = msg[j, rows, 2 * R : 2 * R + 128].astype(F32)
        csum[rows, :] += c
        from_down = jnp.dot(
            msg[j, rows, 0:R], mat[j, 0].reshape(R, R), preferred_element_type=F32
        )
        from_up = jnp.dot(
            msg[j, rows, R : 2 * R], mat[j, 1].reshape(R, R), preferred_element_type=F32
        )
        both = jnp.concatenate([c, c], axis=1)
        gacc[rows, :] += from_down + from_up - both * hup[rows, :]

    def arrive(t, carry):
        j = NS - 1 - t
        for u in (0, 1):
            receive(j, u)
        accumulate(j, slice(0, TOK))
        return carry

    lax.fori_loop(0, NS - 2 - s, arrive, 0)

    for u in (0, 1):
        rows = slice(u * HT, (u + 1) * HT)

        @pl.when(s < NS - 1)
        def _(u=u, rows=rows):
            receive(s + 1, u)
            accumulate(s + 1, rows)

        pre = prebuf[rows, :]
        sig = jax.nn.sigmoid(pre)
        inv = invbuf[rows, 0:1]
        wide = gacc[rows, :] * sig * (1.0 + pre * (1.0 - sig))
        scaled = (wide * inv).astype(BF16)
        pgbuf[rows, :] = scaled

        @pl.when(s > 0)
        def _(u=u, rows=rows, pre=pre, inv=inv, wide=wide, scaled=scaled):
            coef = inv * inv * (jnp.sum(wide * pre, axis=-1, keepdims=True) * (1.0 / D))
            msg[s, rows, 0:R] = scaled
            msg[s, rows, R : 2 * R] = (actbuf[rows, :].astype(F32) * (-csum[rows, 0:1])).astype(BF16)
            msg[s, rows, 2 * R : 2 * R + 128] = jnp.broadcast_to(coef, (HT, 128)).astype(BF16)
            b_copy(s, u).start()

    pgt = pgbuf[...].astype(F32).T
    position = lax.broadcasted_iota(jnp.int32, (1, TOK), 1)
    start = jnp.int32(0)
    for j in range(4):
        end = start + lens[0, j]
        inside = (position >= start) & (position < end)
        masked[j * R : (j + 1) * R, :] = jnp.where(inside, pgt, 0.0).astype(BF16)
        start = end

    def square(count, where):
        def one(t, carry):
            a, b = where(t)
            cols = pl.ds(pl.multiple_of((a * NZ + b) * B, B), B)
            p = jnp.dot(masked[...], nbuf[:, cols], preferred_element_type=F32)
            p = p * p
            fsum[a, b] = (p[0:R] + p[R : 2 * R]) + (p[2 * R : 3 * R] + p[3 * R : 4 * R])
            return carry

        lax.fori_loop(0, count, one, 0)

    rcount = [0]
    rchan = {}

    def rnumber(key):
        if key not in rchan:
            rchan[key] = rcount[0]
            rcount[0] += 1
        return rchan[key]

    def r_copy(key, src, dst, axis, d):
        k = rnumber(key)
        return pltpu.make_async_remote_copy(
            src_ref=src, dst_ref=dst, send_sem=ssem.at[k], recv_sem=rrecv.at[k],
            device_id=hop(axis, d), device_id_type=MESH,
        )

    def go(c):
        c.start()
        sent.append(c)

    def side(d):
        return 0 if d > 0 else 1


    def ring(key, axis, depth, mine, sbuf, rbuf, d, j):
        e = side(d)
        value = mine(j * d)
        m = value.shape[0] // 2
        part = slice(0, m) if d > 0 else slice(m, 2 * m)
        HALF, FULL = pl.ds(0, m), pl.ds(0, 2 * m)
        span = HALF if j == depth else FULL
        if j == depth:
            sbuf[e, j - 1, 0:m] = value[part].astype(BF16)
        else:
            if j == depth - 1:
                r_copy(key + (d, j + 1), sbuf.at[e, j, HALF], rbuf.at[e, j, HALF], axis, d).wait_recv()
                got = rbuf[e, j, 0:m].astype(F32)
                keep = slice(m - part.start, 2 * m - part.start)
                sbuf[e, j - 1, part] = (value[part] + got).astype(BF16)
                sbuf[e, j - 1, keep] = value[keep].astype(BF16)
            else:
                r_copy(key + (d, j + 1), sbuf.at[e, j, FULL], rbuf.at[e, j, FULL], axis, d).wait_recv()
                sbuf[e, j - 1] = (value + rbuf[e, j].astype(F32)).astype(BF16)
        go(r_copy(key + (d, j), sbuf.at[e, j - 1, span], rbuf.at[e, j - 1, span], axis, d))

    def ring_end(key, axis, mine, sbuf, rbuf):
        value = mine(0)
        FULL = pl.ds(0, value.shape[0])
        for d in (1, -1):
            e = side(d)
            r_copy(key + (d, 1), sbuf.at[e, 0, FULL], rbuf.at[e, 0, FULL], axis, d).wait_recv()
            value = value + rbuf[e, 0].astype(F32)
        return value

    def stage_a(q, d, j):
        ring(("A1", q), "x", 2, lambda k: fsum[xo(k), q, 0:XROWS], ra_s.at[q], ra_r.at[q], d, j)

    def stage_b(c, d, j):
        ring(("B1", c), "z", 4, lambda k: fsum[c, zo(k), XROWS:R], rb_s.at[c], rb_r.at[c], d, j)

    square(4, lambda t: (t, zo(4)))
    for c in range(NX):
        for d in (1, -1):
            stage_b(c, d, 4)
    square(7, lambda t: (xo(2), zo(5 + t)))
    for q in range(NZ):
        for d in (1, -1):
            stage_a(q, d, 2)
    square(6, lambda t: (xo(3 + lax.rem(t, 3)), zo(3 + 2 * (t // 3))))
    for c in range(NX):
        for d in (1, -1):
            stage_b(c, d, 3)
    square(10, lambda t: (xo(1 + 2 * (t // 5)), zo(6 + lax.rem(t, 5))))
    for q in range(NZ):
        for d in (1, -1):
            stage_a(q, d, 1)
    square(5, lambda t: (x, zo(6 + t)))
    for c in range(NX):
        for d in (1, -1):
            stage_b(c, d, 2)
    for c in range(NX):
        for d in (1, -1):
            stage_b(c, d, 1)
    for q in range(NZ):
        ga[q] = ring_end(("A1", q), "x", lambda k: fsum[xo(k), q, 0:XROWS], ra_s.at[q], ra_r.at[q])

    def last_a(d, j):
        ring(("A2",), "z", 4, lambda k: ga[zo(k)], sa_s, sa_r, d, j)

    def last_b(d, j):
        ring(("B2",), "x", 2, lambda k: gb[xo(k)], sb_s, sb_r, d, j)

    for d in (1, -1):
        last_a(d, 4)
    for c in range(NX):
        gb[c] = ring_end(("B1", c), "z", lambda k: fsum[c, zo(k), XROWS:R], rb_s.at[c], rb_r.at[c])
    for d in (1, -1):
        last_b(d, 2)
    for d in (1, -1):
        last_a(d, 3)
    for d in (1, -1):
        last_b(d, 1)
    for j in (2, 1):
        for d in (1, -1):
            last_a(d, j)
    low = ring_end(("A2",), "z", lambda k: ga[zo(k)], sa_s, sa_r)
    high = ring_end(("B2",), "x", lambda k: gb[xo(k)], sb_s, sb_r)
    scale = 1.0 / (TOK * NX * NZ)
    out[0] = jnp.concatenate([low, high], axis=0).T * scale
    for c in sent:
        c.wait_send()

    exchange_sent()

    @pl.when(s < NS - 1)
    def _():
        @pl.loop(0, NM)
        def _(i):
            for q in range(NC):
                f_copy(i, q).wait_send()

    @pl.when(s > 0)
    def _():
        def done(t, carry):
            for u in (0, 1):
                b_copy(s + t, u).wait_send()
            return carry

        lax.fori_loop(0, NS - s, done, 0)

        @pl.when(odd == 1)
        def _():
            e_copy(s, s - 1).wait_send()

        def offered(t, carry):
            e_copy(s, s - 1 - odd - 2 * t).wait_send()
            return carry

        lax.fori_loop(0, s // 2, offered, 0)

    @pl.when(odd == 1)
    def _():
        handed()


def per_device(tokens, cotangent, down_weight, up_weight, norm_gain, lengths):
    hbm = pl.BlockSpec(memory_space=pl.ANY)
    vmem = pl.BlockSpec(memory_space=pltpu.VMEM)
    dma = pltpu.SemaphoreType.DMA
    return pl.pallas_call(
        kernel,
        out_shape=jax.ShapeDtypeStruct((1, B, R), F32),
        in_specs=[hbm, hbm, hbm, hbm, vmem, pl.BlockSpec(memory_space=pltpu.SMEM)],
        out_specs=vmem,
        scratch_shapes=[
            pltpu.VMEM((NX, NZ, 2 * B, R), BF16),
            pltpu.VMEM((TOK, D), BF16),
            pltpu.VMEM((TOK, D), BF16),
            pltpu.VMEM((TOK, D), BF16),
            pltpu.VMEM((TOK, D), BF16),
            pltpu.VMEM((NS, 16, D), BF16),
            pltpu.VMEM((NS, 2, NX, NZ, 8, R), BF16),
            pltpu.VMEM((NS, TOK, 2 * R + 128), BF16),
            pltpu.VMEM((TOK, R), F32),
            pltpu.VMEM((TOK, R), F32),
            pltpu.VMEM((TOK, 128), F32),
            pltpu.VMEM((TOK, R), BF16),
            pltpu.VMEM((TOK, R), F32),
            pltpu.VMEM((TOK, 128), F32),
            pltpu.VMEM((TOK, R), BF16),
            pltpu.VMEM((4 * R, TOK), BF16),
            pltpu.VMEM((NX, NZ, R, B), F32),
            pltpu.VMEM((NX, 2, 4, R - XROWS, B), BF16),
            pltpu.VMEM((NX, 2, 4, R - XROWS, B), BF16),
            pltpu.VMEM((NZ, 2, 2, XROWS, B), BF16),
            pltpu.VMEM((NZ, 2, 2, XROWS, B), BF16),
            pltpu.VMEM((NX, R - XROWS, B), F32),
            pltpu.VMEM((NZ, XROWS, B), F32),
            pltpu.VMEM((2, 2, R - XROWS, B), BF16),
            pltpu.VMEM((2, 2, R - XROWS, B), BF16),
            pltpu.VMEM((2, 4, XROWS, B), BF16),
            pltpu.VMEM((2, 4, XROWS, B), BF16),
            dma((4,)),
            dma((GATHER_CHANNELS,)),
            dma((GATHER_CHANNELS,)),
            dma((NM, NC)),
            dma((NS, 2)),
            dma((RS_CHANNELS,)),
            dma((NM, NC)),
            dma((NS, 2)),
            dma((NS,)),
            dma((NS,)),
            dma((NS,)),
            dma((NS, 8)),
            dma((NS, 8)),
            dma((NS, 4)),
            dma((NS, 4)),
        ],
        compiler_params=pltpu.CompilerParams(
            collective_id=0, has_side_effects=True, vmem_limit_bytes=62 * 1024 * 1024
        ),
    )(
        tokens,
        cotangent,
        down_weight[0],
        up_weight[0],
        norm_gain,
        lengths,
    )


def solution(mesh):
    split = Mesh(mesh.devices.reshape(NS, NX, NZ), ("section", "x", "z"))
    dp = ("x", "z")
    return jax.shard_map(
        per_device,
        mesh=split,
        in_specs=(
            P(dp, None),
            P(dp, None),
            P("section", dp, None),
            P("section", dp, None),
            P("section", None),
            P(dp, None),
        ),
        out_specs=P("section", dp, None),
        check_vma=False,
    )
```

```python
import functools

import jax
import jax.numpy as jnp
from jax import lax
from jax.experimental import pallas as pl
from jax.experimental.pallas import tpu as pltpu
from jax.sharding import Mesh
from jax.sharding import PartitionSpec as P

MESH = pl.DeviceIdType.MESH
F32 = jnp.float32
BF16 = jnp.bfloat16
NX, NZ, NS = 4, 8, 8
B = 256
D = 8192
R = 256
TOK = 128
MB = 16
XROWS = 128
NC = 4
PER = NX * NZ // NC
NM = TOK // MB
EPS = 1e-05

GATHER_CHANNELS = 76
RS_CHANNELS = 76


CUT = 304


def half_z(d):
    return pl.ds(0, 160) if d > 0 else pl.ds(160, CUT - 160)


def half_x(d):
    return pl.ds(CUT, 112) if d > 0 else pl.ds(CUT + 112, 96)


ZFIRST, XFIRST = pl.ds(0, CUT), pl.ds(CUT, 2 * B - CUT)


def kernel(
    tok, cot, dwn, upw, gain, lens, out,
    w, hbuf, hout, nbuf, cbuf, ebuf, mat, msg, gacc, hup, csum, actbuf, prebuf, invbuf, pgbuf, masked, fsum,
    rb_s, rb_r, ra_s, ra_r, gb, ga, sb_s, sb_r, sa_s, sa_r,
    lsem, ssem, grecv, frecv, brecv, rrecv, psem, bsend, esend, erecv, hsend, zsend, zrecv, xsend, xrecv,
):
    s = lax.axis_index("section")
    x = lax.axis_index("x")
    z = lax.axis_index("z")

    def xo(k):
        return lax.rem(x + k + NX, NX)

    def zo(k):
        return lax.rem(z + k + NZ, NZ)

    own = (
        pltpu.make_async_copy(dwn, w.at[x, z, pl.ds(B, B)], lsem.at[0]),
        pltpu.make_async_copy(upw, w.at[x, z, pl.ds(0, B)], lsem.at[1]),
    )
    for c in own:
        c.start()

    barrier = pltpu.get_barrier_semaphore()
    s_next, s_prev = lax.rem(s + 1, NS), lax.rem(s + NS - 1, NS)
    for where in (
        {"x": xo(1)}, {"x": xo(-1)}, {"z": zo(1)}, {"z": zo(-1)},
        *({"section": lax.rem(s + k, NS)} for k in range(1, NS)),
    ):
        pl.semaphore_signal(barrier, inc=1, device_id=where, device_id_type=MESH)
    pl.semaphore_wait(barrier, 3 + NS)

    for c in own:
        c.wait()

    first = pltpu.make_async_copy(tok, hbuf, lsem.at[2])
    cotangent = pltpu.make_async_copy(cot, cbuf, lsem.at[3])
    cotangent.start()

    def clear(j, carry):
        ebuf[j] = jnp.zeros((16, D), BF16)
        return carry

    lax.fori_loop(0, s + 1, clear, 0)

    @pl.when(s == 0)
    def _():
        first.start()

    sent = []
    counter = [0]
    chan = {}

    def number(key):
        if key not in chan:
            chan[key] = counter[0]
            counter[0] += 1
        return chan[key]

    def hop(axis, d):
        return {"x": xo(d)} if axis == "x" else {"z": zo(d)}

    def g_send(key, block, axis, d):
        k = number(key)
        c = pltpu.make_async_remote_copy(
            src_ref=block, dst_ref=block, send_sem=ssem.at[k], recv_sem=grecv.at[k],
            device_id=hop(axis, d), device_id_type=MESH,
        )
        c.start()
        sent.append(c)

    def g_wait(key, block, axis, d):
        k = number(key)
        pltpu.make_async_remote_copy(
            src_ref=block, dst_ref=block, send_sem=ssem.at[k], recv_sem=grecv.at[k],
            device_id=hop(axis, d), device_id_type=MESH,
        ).wait_recv()

    XOFF = (0, -1, 1, 2)
    ZOFF = (0, -1, 1, -2, 2, -3, 3, 4)

    def send_dx():
        for d in (1, -1):
            g_send(("dX", d), w.at[x, z, XFIRST], "x", d)

    def wait_dx():
        for d in (1, -1):
            g_wait(("dX", d), w.at[xo(-d), z, XFIRST], "x", d)

    def send_dx2():
        for d in (1, -1):
            g_send(("dX2", d), w.at[xo(-d), z, half_x(d)], "x", d)

    def wait_dx2():
        for d in (1, -1):
            g_wait(("dX2", d), w.at[xo(2), z, half_x(d)], "x", d)

    def send_uz(j):
        for d in (1, -1):
            rows = ZFIRST if j < 4 else half_z(d)
            g_send(("uZ", d, j), w.at[x, zo(-d * (j - 1)), rows], "z", d)

    def wait_uz(j):
        for d in (1, -1):
            rows = ZFIRST if j < 4 else half_z(d)
            g_wait(("uZ", d, j), w.at[x, zo(-d * j), rows], "z", d)

    def send_dz(j, c):
        for d in (1, -1):
            rows = XFIRST if j < 4 else half_x(d)
            g_send(("dZ", d, j, c), w.at[xo(XOFF[c]), zo(-d * (j - 1)), rows], "z", d)

    def wait_dz(j, c):
        for d in (1, -1):
            rows = XFIRST if j < 4 else half_x(d)
            g_wait(("dZ", d, j, c), w.at[xo(XOFF[c]), zo(-d * j), rows], "z", d)

    def send_ux(q):
        for d in (1, -1):
            g_send(("uX", d, q), w.at[x, zo(ZOFF[q]), ZFIRST], "x", d)

    def wait_ux(q):
        for d in (1, -1):
            g_wait(("uX", d, q), w.at[xo(-d), zo(ZOFF[q]), ZFIRST], "x", d)

    def send_ux2(q):
        for d in (1, -1):
            g_send(("uX2", d, q), w.at[xo(-d), zo(ZOFF[q]), half_z(d)], "x", d)

    def wait_ux2(q):
        for d in (1, -1):
            g_wait(("uX2", d, q), w.at[xo(2), zo(ZOFF[q]), half_z(d)], "x", d)

    def relay_ux(q):
        wait_ux(q)
        send_ux2(q)

    def relay_dz(j, c):
        wait_dz(j, c)
        send_dz(j + 1, c)

    send_dx()
    send_uz(1)
    send_dz(1, 0)
    send_ux(0)
    wait_dx()
    send_dx2()
    send_dz(1, 1)
    send_dz(1, 2)
    wait_uz(1)
    send_uz(2)
    send_ux(1)
    send_ux(2)
    wait_dx2()
    send_dz(1, 3)
    relay_ux(0)
    relay_dz(1, 0)
    wait_uz(2)
    send_uz(3)
    send_ux(3)
    send_ux(4)
    relay_ux(1)
    relay_ux(2)
    relay_dz(1, 1)
    relay_dz(1, 2)
    wait_uz(3)
    send_uz(4)
    send_ux(5)
    send_ux(6)
    relay_dz(1, 3)
    relay_dz(2, 0)
    relay_ux(3)
    relay_ux(4)
    relay_dz(2, 1)
    relay_dz(2, 2)
    wait_uz(4)
    send_ux(7)
    relay_dz(2, 3)
    relay_ux(5)
    relay_ux(6)
    for c in range(4):
        relay_dz(3, c)
    relay_ux(7)
    for c in range(4):
        wait_dz(4, c)
    for q in range(8):
        wait_ux2(q)
    for c in sent:
        c.wait_send()
    sent.clear()

    @pl.when(s == 0)
    def _():
        first.wait()

    LATE = 4
    begin_at = jnp.where(s >= 5, -1, jnp.where(s == 4, 5, jnp.where(s == 3, 7, NM)))
    hand_at = jnp.where(s >= 5, -1, jnp.where(s == 3, 6, NM - 1))

    def blk(r):
        return slice(r * B, (r + 1) * B)

    replica = x * NZ + z
    odd = lax.rem(s, 2)

    def e_copy(j, below):
        return pltpu.make_async_remote_copy(
            src_ref=ebuf.at[j], dst_ref=ebuf.at[j], send_sem=esend.at[below], recv_sem=erecv.at[j],
            device_id={"section": below}, device_id_type=MESH,
        )

    @pl.when(s > 0)
    def _():
        pick = lax.broadcasted_iota(jnp.int32, (8, R), 1) == (
            lax.broadcasted_iota(jnp.int32, (8, R), 0) + replica * 8
        )
        pick = jnp.where(pick, 1.0, 0.0).astype(BF16)
        for r in range(NX * NZ):
            rows_d = lax.dot_general(
                pick, w[r // NZ, r % NZ, B : 2 * B], (((1,), (1,)), ((), ())), preferred_element_type=F32
            )
            rows_u = lax.dot_general(
                pick, w[r // NZ, r % NZ, 0:B], (((1,), (1,)), ((), ())), preferred_element_type=F32
            )
            ebuf[s, :, blk(r)] = jnp.concatenate([rows_d * gain[:, blk(r)], rows_u], axis=0).astype(BF16)

        @pl.when(odd == 1)
        def _():
            e_copy(s, s - 1).start()

        def offer(t, carry):
            e_copy(s, s - 1 - odd - 2 * t).start()
            return carry

        lax.fori_loop(0, s // 2, offer, 0)

    def z_copy(j, h, d, arriving):
        k = zo(-d * h) if arriving else zo(-d * (h - 1))
        e = 0 if d > 0 else 1
        ref = mat.at[j, :, x, k] if h < 4 else mat.at[j, e, x, k]
        return pltpu.make_async_remote_copy(
            src_ref=ref, dst_ref=ref, send_sem=zsend.at[j, 2 * h - 2 + e], recv_sem=zrecv.at[j, 2 * h - 2 + e],
            device_id={"z": zo(d)}, device_id_type=MESH,
        )

    def x_copy(j, h, d, arriving):
        k = xo(-d * h) if arriving else xo(-d * (h - 1))
        e = 0 if d > 0 else 1
        ref = mat.at[j, :, k] if h < 2 else mat.at[j, e, k]
        return pltpu.make_async_remote_copy(
            src_ref=ref, dst_ref=ref, send_sem=xsend.at[j, 2 * h - 2 + e], recv_sem=xrecv.at[j, 2 * h - 2 + e],
            device_id={"x": xo(d)}, device_id_type=MESH,
        )

    def above(body):
        def step(t, carry):
            body(s + 1 + t)
            return carry

        lax.fori_loop(0, NS - 1 - s, step, 0)

    def hand_on():
        def one(j):
            e_copy(j, s_prev).wait_recv()
            pltpu.make_async_remote_copy(
                src_ref=ebuf.at[j], dst_ref=ebuf.at[j], send_sem=hsend.at[j], recv_sem=erecv.at[j],
                device_id={"section": s_prev}, device_id_type=MESH,
            ).start()

        above(one)

    def handed():
        above(lambda j: pltpu.make_async_remote_copy(
            src_ref=ebuf.at[j], dst_ref=ebuf.at[j], send_sem=hsend.at[j], recv_sem=erecv.at[j],
            device_id={"section": s_prev}, device_id_type=MESH,
        ).wait_send())

    def exchange_begin():
        @pl.when(odd == 0)
        def _():
            above(lambda j: e_copy(j, s_prev).wait_recv())

        acc = jnp.zeros((NS * 16, R), F32)
        for r in range(NX * NZ):
            rows_e = ebuf[:, :, blk(r)].reshape(NS * 16, B)
            acc = acc + jnp.dot(rows_e, w[r // NZ, r % NZ, 0:B], preferred_element_type=F32)
        for j in range(1, NS):
            mat[j, 0, x, z] = acc[16 * j : 16 * j + 8].astype(BF16)
            mat[j, 1, x, z] = acc[16 * j + 8 : 16 * j + 16].astype(BF16)

        def begin(j):
            for d in (1, -1):
                z_copy(j, 1, d, False).start()

        above(begin)

    def along(h):
        def on(j):
            for d in (1, -1):
                z_copy(j, h, d, True).wait_recv()
            for d in (1, -1):
                z_copy(j, h + 1, d, False).start()

        above(on)

    def turn():
        def one(j):
            for d in (1, -1):
                z_copy(j, 4, d, True).wait_recv()
            for d in (1, -1):
                x_copy(j, 1, d, False).start()

        above(one)

    def across():
        def one(j):
            for d in (1, -1):
                x_copy(j, 1, d, True).wait_recv()
            for d in (1, -1):
                x_copy(j, 2, d, False).start()

        above(one)

    def finish():
        def one(j):
            for d in (1, -1):
                x_copy(j, 2, d, True).wait_recv()

        above(one)

    exchange_steps = (
        lambda: along(1), lambda: along(2), lambda: along(3), turn, across, finish,
    )

    def exchange_sent():
        def one(j):
            for d in (1, -1):
                for h in (1, 2, 3, 4):
                    z_copy(j, h, d, False).wait_send()
                for h in (1, 2):
                    x_copy(j, h, d, False).wait_send()

        above(one)

    def start_gradient():
        cotangent.wait()
        acc = jnp.zeros((TOK, R), F32)
        for r in range(NX * NZ):
            acc = acc + jnp.dot(cbuf[:, blk(r)], w[r // NZ, r % NZ, 0:B], preferred_element_type=F32)
        gacc[...] = acc

    @pl.when(s >= LATE)
    def _():
        start_gradient()

    @pl.when((odd == 1) & (hand_at < 0))
    def _():
        hand_on()

    @pl.when((begin_at < 0) & (s < NS - 1))
    def _():
        exchange_begin()

    def micro(i):
        return pl.ds(pl.multiple_of(i * MB, MB), MB)

    def f_copy(i, q):
        cols = pl.ds(q * PER * B, PER * B)
        return pltpu.make_async_remote_copy(
            src_ref=hout.at[micro(i), cols], dst_ref=hbuf.at[micro(i), cols],
            send_sem=psem.at[i, q], recv_sem=frecv.at[i, q],
            device_id={"section": s_next}, device_id_type=MESH,
        )

    def forward(i, carry):
        rows = micro(i)
        squares = jnp.zeros((MB, B), F32)
        accs = [jnp.zeros((MB, 128), F32)] * 2
        for q in range(NC):
            @pl.when(s > 0)
            def _(q=q):
                f_copy(i, q).wait_recv()

            for r in range(q * PER, (q + 1) * PER):
                h = hbuf[rows, blk(r)].astype(F32)
                squares = squares + h * h
                n = (h * gain[:, blk(r)]).astype(BF16)
                nbuf[rows, blk(r)] = n
                for e in range(2):
                    cut = w[r // NZ, r % NZ, B : 2 * B, e * 128 : (e + 1) * 128]
                    accs[e] = accs[e] + jnp.dot(n, cut, preferred_element_type=F32)
        inv = lax.rsqrt(jnp.sum(squares, axis=-1, keepdims=True) * (1.0 / D) + EPS)
        acc = jnp.concatenate(accs, axis=1) * inv
        prebuf[rows, :] = acc
        invbuf[rows, :] = jnp.broadcast_to(inv, (MB, 128))
        act = (acc * jax.nn.sigmoid(acc)).astype(BF16)
        actbuf[rows, :] = act

        @pl.when(s < NS - 1)
        def _():
            for q in range(NC):
                for r in range(q * PER, (q + 1) * PER):
                    up = lax.dot_general(
                        act, w[r // NZ, r % NZ, 0:B], (((1,), (1,)), ((), ())), preferred_element_type=F32
                    )
                    hout[rows, blk(r)] = (hbuf[rows, blk(r)].astype(F32) + up).astype(BF16)
                f_copy(i, q).start()

        @pl.when((odd == 1) & (i == hand_at))
        def _():
            hand_on()

        @pl.when(s < NS - 1)
        def _():
            pl.when(i == begin_at)(exchange_begin)
            for k, step in enumerate(exchange_steps):
                pl.when(i == begin_at + 1 + k)(step)

        return carry

    lax.fori_loop(0, NM, forward, 0)

    @pl.when(begin_at >= NM)
    def _():
        exchange_begin()

    @pl.when(s < LATE)
    def _():
        start_gradient()

    @pl.when(s < NS - 1)
    def _():
        acc = jnp.zeros((TOK, R), F32)
        for r in range(NX * NZ):
            acc = acc + jnp.dot(hout[:, blk(r)], w[r // NZ, r % NZ, 0:B], preferred_element_type=F32)
        hup[...] = acc
        for k, step in enumerate(exchange_steps):
            pl.when(begin_at + 1 + k >= NM)(step)

    csum[...] = jnp.zeros((TOK, 128), F32)

    HT = TOK // 2

    def b_copy(j, u):
        part = msg.at[j, pl.ds(u * HT, HT)]
        return pltpu.make_async_remote_copy(
            src_ref=part, dst_ref=part, send_sem=bsend.at[j, u], recv_sem=brecv.at[j, u],
            device_id={"section": s_prev}, device_id_type=MESH,
        )

    def receive(j, u):
        b_copy(j, u).wait_recv()

        @pl.when(s > 0)
        def _():
            b_copy(j, u).start()

    def accumulate(j, rows):
        c = msg[j, rows, 2 * R : 2 * R + 128].astype(F32)
        csum[rows, :] += c
        from_down = jnp.dot(
            msg[j, rows, 0:R], mat[j, 0].reshape(R, R), preferred_element_type=F32
        )
        from_up = jnp.dot(
            msg[j, rows, R : 2 * R], mat[j, 1].reshape(R, R), preferred_element_type=F32
        )
        both = jnp.concatenate([c, c], axis=1)
        gacc[rows, :] += from_down + from_up - both * hup[rows, :]

    def arrive(t, carry):
        j = NS - 1 - t
        for u in (0, 1):
            receive(j, u)
        accumulate(j, slice(0, TOK))
        return carry

    lax.fori_loop(0, NS - 2 - s, arrive, 0)

    for u in (0, 1):
        rows = slice(u * HT, (u + 1) * HT)

        @pl.when(s < NS - 1)
        def _(u=u, rows=rows):
            receive(s + 1, u)
            accumulate(s + 1, rows)

        pre = prebuf[rows, :]
        sig = jax.nn.sigmoid(pre)
        inv = invbuf[rows, 0:1]
        wide = gacc[rows, :] * sig * (1.0 + pre * (1.0 - sig))
        scaled = (wide * inv).astype(BF16)
        pgbuf[rows, :] = scaled

        @pl.when(s > 0)
        def _(u=u, rows=rows, pre=pre, inv=inv, wide=wide, scaled=scaled):
            coef = inv * inv * (jnp.sum(wide * pre, axis=-1, keepdims=True) * (1.0 / D))
            msg[s, rows, 0:R] = scaled
            msg[s, rows, R : 2 * R] = (actbuf[rows, :].astype(F32) * (-csum[rows, 0:1])).astype(BF16)
            msg[s, rows, 2 * R : 2 * R + 128] = jnp.broadcast_to(coef, (HT, 128)).astype(BF16)
            b_copy(s, u).start()

    pgt = pgbuf[...].astype(F32).T
    position = lax.broadcasted_iota(jnp.int32, (1, TOK), 1)
    start = jnp.int32(0)
    for j in range(4):
        end = start + lens[0, j]
        inside = (position >= start) & (position < end)
        masked[j * R : (j + 1) * R, :] = jnp.where(inside, pgt, 0.0).astype(BF16)
        start = end

    def square(count, where):
        def one(t, carry):
            a, b = where(t)
            cols = pl.ds(pl.multiple_of((a * NZ + b) * B, B), B)
            p = jnp.dot(masked[...], nbuf[:, cols], preferred_element_type=F32)
            p = p * p
            fsum[a, b] = (p[0:R] + p[R : 2 * R]) + (p[2 * R : 3 * R] + p[3 * R : 4 * R])
            return carry

        lax.fori_loop(0, count, one, 0)

    rcount = [0]
    rchan = {}

    def rnumber(key):
        if key not in rchan:
            rchan[key] = rcount[0]
            rcount[0] += 1
        return rchan[key]

    def r_copy(key, src, dst, axis, d):
        k = rnumber(key)
        return pltpu.make_async_remote_copy(
            src_ref=src, dst_ref=dst, send_sem=ssem.at[k], recv_sem=rrecv.at[k],
            device_id=hop(axis, d), device_id_type=MESH,
        )

    def go(c):
        c.start()
        sent.append(c)

    def side(d):
        return 0 if d > 0 else 1


    def ring(key, axis, depth, mine, sbuf, rbuf, d, j):
        e = side(d)
        value = mine(j * d)
        m = value.shape[0] // 2
        part = slice(0, m) if d > 0 else slice(m, 2 * m)
        HALF, FULL = pl.ds(0, m), pl.ds(0, 2 * m)
        span = HALF if j == depth else FULL
        if j == depth:
            sbuf[e, j - 1, 0:m] = value[part].astype(BF16)
        else:
            if j == depth - 1:
                r_copy(key + (d, j + 1), sbuf.at[e, j, HALF], rbuf.at[e, j, HALF], axis, d).wait_recv()
                got = rbuf[e, j, 0:m].astype(F32)
                keep = slice(m - part.start, 2 * m - part.start)
                sbuf[e, j - 1, part] = (value[part] + got).astype(BF16)
                sbuf[e, j - 1, keep] = value[keep].astype(BF16)
            else:
                r_copy(key + (d, j + 1), sbuf.at[e, j, FULL], rbuf.at[e, j, FULL], axis, d).wait_recv()
                sbuf[e, j - 1] = (value + rbuf[e, j].astype(F32)).astype(BF16)
        go(r_copy(key + (d, j), sbuf.at[e, j - 1, span], rbuf.at[e, j - 1, span], axis, d))

    def ring_end(key, axis, mine, sbuf, rbuf):
        value = mine(0)
        FULL = pl.ds(0, value.shape[0])
        for d in (1, -1):
            e = side(d)
            r_copy(key + (d, 1), sbuf.at[e, 0, FULL], rbuf.at[e, 0, FULL], axis, d).wait_recv()
            value = value + rbuf[e, 0].astype(F32)
        return value

    def stage_a(q, d, j):
        ring(("A1", q), "x", 2, lambda k: fsum[xo(k), q, 0:XROWS], ra_s.at[q], ra_r.at[q], d, j)

    def stage_b(c, d, j):
        ring(("B1", c), "z", 4, lambda k: fsum[c, zo(k), XROWS:R], rb_s.at[c], rb_r.at[c], d, j)

    square(4, lambda t: (t, zo(4)))
    for c in range(NX):
        for d in (1, -1):
            stage_b(c, d, 4)
    square(7, lambda t: (xo(2), zo(5 + t)))
    for q in range(NZ):
        for d in (1, -1):
            stage_a(q, d, 2)
    square(6, lambda t: (xo(3 + lax.rem(t, 3)), zo(3 + 2 * (t // 3))))
    for c in range(NX):
        for d in (1, -1):
            stage_b(c, d, 3)
    square(10, lambda t: (xo(1 + 2 * (t // 5)), zo(6 + lax.rem(t, 5))))
    for q in range(NZ):
        for d in (1, -1):
            stage_a(q, d, 1)
    square(5, lambda t: (x, zo(6 + t)))
    for c in range(NX):
        for d in (1, -1):
            stage_b(c, d, 2)
    for c in range(NX):
        for d in (1, -1):
            stage_b(c, d, 1)
    for q in range(NZ):
        ga[q] = ring_end(("A1", q), "x", lambda k: fsum[xo(k), q, 0:XROWS], ra_s.at[q], ra_r.at[q])

    def last_a(d, j):
        ring(("A2",), "z", 4, lambda k: ga[zo(k)], sa_s, sa_r, d, j)

    def last_b(d, j):
        ring(("B2",), "x", 2, lambda k: gb[xo(k)], sb_s, sb_r, d, j)

    for d in (1, -1):
        last_a(d, 4)
    for c in range(NX):
        gb[c] = ring_end(("B1", c), "z", lambda k: fsum[c, zo(k), XROWS:R], rb_s.at[c], rb_r.at[c])
    for d in (1, -1):
        last_b(d, 2)
    for d in (1, -1):
        last_a(d, 3)
    for d in (1, -1):
        last_b(d, 1)
    for j in (2, 1):
        for d in (1, -1):
            last_a(d, j)
    low = ring_end(("A2",), "z", lambda k: ga[zo(k)], sa_s, sa_r)
    high = ring_end(("B2",), "x", lambda k: gb[xo(k)], sb_s, sb_r)
    scale = 1.0 / (TOK * NX * NZ)
    out[0] = jnp.concatenate([low, high], axis=0).T * scale
    for c in sent:
        c.wait_send()

    exchange_sent()

    @pl.when(s < NS - 1)
    def _():
        @pl.loop(0, NM)
        def _(i):
            for q in range(NC):
                f_copy(i, q).wait_send()

    @pl.when(s > 0)
    def _():
        def done(t, carry):
            for u in (0, 1):
                b_copy(s + t, u).wait_send()
            return carry

        lax.fori_loop(0, NS - s, done, 0)

        @pl.when(odd == 1)
        def _():
            e_copy(s, s - 1).wait_send()

        def offered(t, carry):
            e_copy(s, s - 1 - odd - 2 * t).wait_send()
            return carry

        lax.fori_loop(0, s // 2, offered, 0)

    @pl.when(odd == 1)
    def _():
        handed()


def per_device(tokens, cotangent, down_weight, up_weight, norm_gain, lengths):
    hbm = pl.BlockSpec(memory_space=pl.ANY)
    vmem = pl.BlockSpec(memory_space=pltpu.VMEM)
    dma = pltpu.SemaphoreType.DMA
    return pl.pallas_call(
        kernel,
        out_shape=jax.ShapeDtypeStruct((1, B, R), F32),
        in_specs=[hbm, hbm, hbm, hbm, vmem, pl.BlockSpec(memory_space=pltpu.SMEM)],
        out_specs=vmem,
        scratch_shapes=[
            pltpu.VMEM((NX, NZ, 2 * B, R), BF16),
            pltpu.VMEM((TOK, D), BF16),
            pltpu.VMEM((TOK, D), BF16),
            pltpu.VMEM((TOK, D), BF16),
            pltpu.VMEM((TOK, D), BF16),
            pltpu.VMEM((NS, 16, D), BF16),
            pltpu.VMEM((NS, 2, NX, NZ, 8, R), BF16),
            pltpu.VMEM((NS, TOK, 2 * R + 128), BF16),
            pltpu.VMEM((TOK, R), F32),
            pltpu.VMEM((TOK, R), F32),
            pltpu.VMEM((TOK, 128), F32),
            pltpu.VMEM((TOK, R), BF16),
            pltpu.VMEM((TOK, R), F32),
            pltpu.VMEM((TOK, 128), F32),
            pltpu.VMEM((TOK, R), BF16),
            pltpu.VMEM((4 * R, TOK), BF16),
            pltpu.VMEM((NX, NZ, R, B), F32),
            pltpu.VMEM((NX, 2, 4, R - XROWS, B), BF16),
            pltpu.VMEM((NX, 2, 4, R - XROWS, B), BF16),
            pltpu.VMEM((NZ, 2, 2, XROWS, B), BF16),
            pltpu.VMEM((NZ, 2, 2, XROWS, B), BF16),
            pltpu.VMEM((NX, R - XROWS, B), F32),
            pltpu.VMEM((NZ, XROWS, B), F32),
            pltpu.VMEM((2, 2, R - XROWS, B), BF16),
            pltpu.VMEM((2, 2, R - XROWS, B), BF16),
            pltpu.VMEM((2, 4, XROWS, B), BF16),
            pltpu.VMEM((2, 4, XROWS, B), BF16),
            dma((4,)),
            dma((GATHER_CHANNELS,)),
            dma((GATHER_CHANNELS,)),
            dma((NM, NC)),
            dma((NS, 2)),
            dma((RS_CHANNELS,)),
            dma((NM, NC)),
            dma((NS, 2)),
            dma((NS,)),
            dma((NS,)),
            dma((NS,)),
            dma((NS, 8)),
            dma((NS, 8)),
            dma((NS, 4)),
            dma((NS, 4)),
        ],
        compiler_params=pltpu.CompilerParams(
            collective_id=0, has_side_effects=True, vmem_limit_bytes=62 * 1024 * 1024
        ),
    )(
        tokens,
        cotangent,
        down_weight[0],
        up_weight[0],
        norm_gain,
        lengths,
    )


def solution(mesh):
    split = Mesh(mesh.devices.reshape(NS, NX, NZ), ("section", "x", "z"))
    dp = ("x", "z")
    return jax.shard_map(
        per_device,
        mesh=split,
        in_specs=(
            P(dp, None),
            P(dp, None),
            P("section", dp, None),
            P("section", dp, None),
            P("section", None),
            P(dp, None),
        ),
        out_specs=P("section", dp, None),
        check_vma=False,
    )
```
